32 devices in a mesh: dp: 8 (over y, x, core), tensor: 4 (over z).
Axes of the slice: x: 2, y: 2, z: 4, core: 2. Of those that a mesh axis runs over, the one named last changes fastest.
Arguments:
- send_order: int32 [32, 32], P(('dp', 'tensor')), may hold values from 0 to 31, each once within a row
- master: float32 [32, 32, 2048], P(('dp', 'tensor')), may hold values from -6 to 6
- first_code: bfloat16 [32, 32, 2048], P(('dp', 'tensor')), may hold values from -1 to 1
- first_scale: float32 [32, 32], P(('dp', 'tensor')), may hold values from 0.1 to 2
- second_code: bfloat16 [32, 32, 2048], P(('dp', 'tensor')), may hold values from 0.049804688 to 1
- second_scale: float32 [32, 32], P(('dp', 'tensor')), may hold values from 0.5 to 20
- grads: bfloat16 [8, 4, 8, 32, 2048], P('dp', 'tensor'), may hold values from -6 to 6
Outputs:
- new_master: float32 [32, 32, 2048], P(('dp', 'tensor'))
- new_first_code: bfloat16 [32, 32, 2048], P(('dp', 'tensor'))
- new_first_scale: float32 [32, 32], P(('dp', 'tensor'))
- new_second_code: bfloat16 [32, 32, 2048], P(('dp', 'tensor'))
- new_second_scale: float32 [32, 32], P(('dp', 'tensor'))
- weights: bfloat16 [4, 8, 32, 2048], P('tensor')
The draws below stay inside these ranges and needn't reach their ends.
Inputs may be any that keep to these rules, and one draw needn't show every extreme that they name: `send_order`: each row is an ordering of the slots 0 to 31, each once.
All inputs are finite; a program needn't handle non-finite values. Where the reference program divides by a largest or mean magnitude, that divisor is 1e-20 or more.
Results may differ from the reference program's by a relative error of at most 0.001.
Values may be sent and summed in bfloat16 or wider, within the bound.
A program may use at most 128 MiB of HBM per device.

```python
import math
import jax
import jax.numpy as jnp
from jax import lax

BLOCK = 2048
PER = 1
BPD = 32
STEP = 10
N_DP = 8
N_TENSOR = 4
DEVICES = 32


def raised(values, rng, source, target, blocks, factor):
    def block_of(dim):
        return (jnp.arange(values.shape[dim]) // (values.shape[dim] // blocks)).reshape((-1,) + (1,) * (values.ndim - 1 - dim))

    one_side = jax.random.permutation(rng, blocks)[block_of(target)]
    second = (block_of(target) + blocks // 2) % blocks
    return jnp.where((block_of(source) == one_side) | (block_of(source) == second), factor * values, values)


def block_scale(own_key, dims, pieces, smallest, high):
    def one(position, blocks):
        heights = jax.random.uniform(jax.random.fold_in(jax.random.fold_in(own_key, 6), position), (blocks,), jnp.float32, smallest / len(pieces), high / len(pieces))
        return jnp.repeat(jnp.exp(heights), dims[position] // blocks).reshape((-1,) + (1,) * (len(dims) - position - 1))

    level = one(*pieces[0])
    for cut in pieces[1:]:
        level = level * one(*cut)
    return level


def centred(rng, dims, width, most, shards=(), held_as=jnp.bfloat16):
    values = jax.random.normal(rng, dims, jnp.float32) * width
    if len(shards) > 0:
        values = block_scale(rng, dims, shards, -0.22, 0.18) * values
    return jnp.clip(values, min=-most, max=most).astype(held_as)


def noise_with(own_key, extent, spread, bound, shards, heavy, kind=jnp.bfloat16):
    array = spread * jax.random.normal(own_key, extent, jnp.float32)
    if shards:
        array = array * block_scale(own_key, extent, shards, -0.22, 0.18)
    return jnp.clip(raised(array, jax.random.fold_in(own_key, 3), *heavy), -bound, bound).astype(kind)


def setup_inputs(seed: int = 0) -> dict:
    streams_of = jax.random.split(jax.random.key(seed), 8)
    return {
        "send_order": jax.vmap(lambda own: jax.random.permutation(own, BPD))(jax.random.split(streams_of[0], DEVICES)).reshape((DEVICES, BPD)).astype(jnp.int32),
        "master": centred(streams_of[1], (DEVICES, BPD, BLOCK), 1.0, 6.0, ((0, 32),), jnp.float32),
        "first_code": jnp.clip(jax.random.uniform(streams_of[2], (DEVICES, BPD, BLOCK), jnp.float32, -1.0, 1.0) * block_scale(streams_of[2], (DEVICES, BPD, BLOCK), ((0, 32),), -0.4, 0.0), -1.0, 1.0).astype(jnp.bfloat16),
        "first_scale": jnp.clip(jnp.exp(math.log(2.0) - 2.9957323 * jax.random.uniform(streams_of[3], (DEVICES, BPD), jnp.float32) ** block_scale(streams_of[3], (DEVICES, BPD), ((0, 32),), -0.2, 0.2)), 0.1, 2.0),
        "second_code": jnp.clip(0.049804688 + 0.9501953 * jax.random.uniform(streams_of[4], (DEVICES, BPD, BLOCK), jnp.float32) ** block_scale(streams_of[4], (DEVICES, BPD, BLOCK), ((0, 32),), -0.2, 0.2), 0.049804688, 1.0).astype(jnp.bfloat16),
        "second_scale": jnp.clip(jnp.exp(math.log(20.0) - 3.6888795 * jax.random.uniform(streams_of[5], (DEVICES, BPD), jnp.float32) ** block_scale(streams_of[5], (DEVICES, BPD), ((0, 32),), -0.2, 0.2)), 0.5, 20.0),
        "grads": noise_with(streams_of[6], (N_DP, N_TENSOR, N_DP, BPD, BLOCK), 1.0, 6.0, ((0, 8), (1, 4)), (0, 2, 8, 2.0)),
    }


def relay_array(source, send_order):
    rows = jnp.arange(DEVICES, dtype=jnp.int32)[:, None]
    taken = source[rows, send_order]
    rest = taken.shape[2:]
    taken = taken.reshape((DEVICES, DEVICES, PER) + rest)
    taken = jnp.swapaxes(taken, 0, 1)
    return taken.reshape((DEVICES, BPD) + rest)

def reference(send_order, master, first_code, first_scale, second_code, second_scale, grads):
    master_new = relay_array(master, send_order)
    code_one = relay_array(first_code, send_order)
    scale_one = relay_array(first_scale, send_order)
    code_two = relay_array(second_code, send_order)
    scale_two = relay_array(second_scale, send_order)

    def accumulate(total, piece):
        return (total + piece.astype(jnp.float32), None)
    start = jnp.zeros(grads.shape[1:], jnp.float32)
    summed, unused = lax.scan(accumulate, start, grads)
    grad = jnp.swapaxes(summed, 0, 1).reshape(DEVICES, BPD, BLOCK)
    first = code_one.astype(jnp.float32) * scale_one[:, :, None]
    second = code_two.astype(jnp.float32) * scale_two[:, :, None]
    moment_one = 0.9 * first + 0.1 * grad
    moment_two = 0.95 * second + 0.05 * grad * grad
    corr_one = 1.0 - 0.9 ** STEP
    corr_two = 1.0 - 0.95 ** STEP
    update = moment_one / corr_one / (jnp.sqrt(moment_two / corr_two) + 1e-08) + 0.1 * master_new
    new_master = master_new - 0.01 * update
    new_scale_one = lax.optimization_barrier(jnp.max(jnp.abs(moment_one), axis=2)) + 1e-06
    new_code_one = (moment_one / new_scale_one[:, :, None]).astype(jnp.bfloat16)
    new_scale_two = lax.optimization_barrier(jnp.max(jnp.abs(moment_two), axis=2)) + 1e-06
    new_code_two = (moment_two / new_scale_two[:, :, None]).astype(jnp.bfloat16)
    weights = new_master.astype(jnp.bfloat16).reshape(N_DP, N_TENSOR, BPD, BLOCK)
    weights = jnp.swapaxes(weights, 0, 1)
    return (new_master, new_code_one, new_scale_one, new_code_two, new_scale_two, weights)
```

```python
from contextlib import nullcontext as span
import functools
import math

import jax
import jax.numpy as jnp
from jax import lax
from jax.experimental import pallas as pl
from jax.experimental.pallas import tpu as pltpu
from jax.sharding import PartitionSpec as P

STEP = 10
LANES = 128
RELAYS = 2
PARTS = 4
LEVELS = 32767.0
TINY = 1e-30
MESH = pl.DeviceIdType.MESH


def _kernel(nd, nt, slots, width, order_hbm, m_hbm, c1_hbm, s1_hbm, c2_hbm, s2_hbm, g_hbm,
            nm_out, nc1_out, ns1_out, nc2_out, ns2_out, wg,
            order_v, s1_v, s2_v, m_v, c1_v, c2_v, xf_m, xf_c,
            xs_m, xs_c, xs_s, xr_m, xr_c, xr_s, own, got,
            keep_x, keep_y, q1_x, q1_y, r1_x, r1_y, q2_x, q2_y, r2_x, r2_y,
            t1_x, t1_y, u1_x, u1_y, t2_x, t2_y, u2_x, u2_y, m1_v, m2_v,
            in_sem, own_sem, rm, rc, rs, sm, sc, ss, rp, sp,
            ra1, sa1, rb1, sb1, ra2, sa2, rb2, sb2, ra, sa, rf, sf):
    n = nd * nt
    per = slots // n
    chunks = width // LANES
    cp = chunks // RELAYS
    cq = chunks // PARTS
    wr = width // RELAYS
    wp = width // PARTS
    ny = nd // 4
    chips = 2 * ny
    my_dp = lax.axis_index("dp")
    my_t = lax.axis_index("tensor")
    me = my_dp * nt + my_t
    my_c = lax.rem(my_dp, 2)
    my_chip = my_dp // 2
    my_x = lax.rem(my_chip, 2)
    my_y = my_chip // 2
    other_c = 1 - my_c
    other_x = 1 - my_x
    partner = my_dp + 1 - 2 * my_c

    def dp_of(y, x, c):
        return (y * 2 + x) * 2 + c

    def row_away(away):
        return lax.rem(my_y + away, ny)

    barrier = pltpu.get_barrier_semaphore()

    def greet(k, carry):
        dst = lax.rem(me + n - k, n)
        pl.semaphore_signal(barrier, inc=1, device_id=(dst // nt, lax.rem(dst, nt)), device_id_type=MESH)
        return carry

    lax.fori_loop(1, n, greet, 0)

    loads = [
        pltpu.make_async_copy(order_hbm, order_v, in_sem.at[0]),
        pltpu.make_async_copy(m_hbm.at[0], m_v, in_sem.at[3]),
        pltpu.make_async_copy(s1_hbm, s1_v, in_sem.at[1]),
        pltpu.make_async_copy(s2_hbm, s2_v, in_sem.at[2]),
        pltpu.make_async_copy(c1_hbm.at[0], c1_v, in_sem.at[4]),
        pltpu.make_async_copy(c2_hbm.at[0], c2_v, in_sem.at[5]),
    ]
    for item in loads:
        item.start()

    load_own = pltpu.make_async_copy(g_hbm.at[:, :, my_c], own, own_sem.at[0])
    load_own.start()

    def cols(h):
        return pl.ds(h * wp, wp)

    def wide(r):
        return pl.ds(r * wr, wr)

    def drain(ref, sem):
        pltpu.make_async_copy(ref, ref, sem).wait()

    with span("loads"):
        for item in loads:
            item.wait()

    eye = lax.broadcasted_iota(jnp.int32, (slots, slots), 0) == lax.broadcasted_iota(jnp.int32, (slots, slots), 1)

    def as_row(col):
        return jnp.sum(jnp.where(eye, col, 0.0), axis=0, keepdims=True)

    def as_col(row):
        return jnp.sum(jnp.where(eye, row, 0.0), axis=1, keepdims=True)

    def scale_of(x):
        return (jnp.max(jnp.abs(x), axis=1, keepdims=True) + TINY) * (1.0 / LEVELS)

    with span("prep"):
        lane = lax.broadcasted_iota(jnp.int32, (slots, slots), 1)
        order_col = as_col(order_v[...].astype(jnp.float32))
        pick = order_col == lane.astype(jnp.float32)

        def picked(row):
            return jnp.sum(jnp.where(pick, row, 0.0), axis=1, keepdims=True)

        m_scale = scale_of(m_v[...])
        m_inv = 1.0 / m_scale
        place = lax.broadcasted_iota(jnp.int32, (slots, LANES), 1)
        both = jnp.where(place < LANES // 4, picked(s1_v[...]), picked(s2_v[...]))
        xs_s[:, 0, :] = jnp.where(place < LANES // 2, both, picked(as_row(m_scale)))
        select = jnp.where(pick, 1.0, 0.0).astype(jnp.bfloat16)

    def take(x):
        return jnp.dot(select, x, preferred_element_type=jnp.float32)

    def stage(r):
        level = jnp.round(m_v[:, wide(r)] * m_inv)
        high = jnp.round(level * (1.0 / 256.0))
        low = level - 256.0 * high
        xm = 256.0 * take(high.astype(jnp.bfloat16)) + take(low.astype(jnp.bfloat16))
        x1 = take(c1_v[:, wide(r)])
        x2 = take(c2_v[:, wide(r)])
        for j in range(cp):
            piece = slice(j * LANES, (j + 1) * LANES)
            xf_m[r, pl.ds(j, slots, stride=cp), :] = xm[:, piece]
            xf_c[r, pl.ds(j, slots, stride=2 * cp), :] = x1[:, piece]
            xf_c[r, pl.ds(cp + j, slots, stride=2 * cp), :] = x2[:, piece]
        xs_m[r] = xf_m[r].reshape(slots, cp, LANES).astype(jnp.int16)
        xs_c[r] = xf_c[r].reshape(slots, 2 * cp, LANES).astype(jnp.bfloat16)

    with span("stage"):
        for r in range(RELAYS):
            stage(r)

    with span("barrier"):
        pl.semaphore_wait(barrier, n - 1)

    def send_pairs(h):
        pltpu.make_async_remote_copy(
            src_ref=g_hbm.at[:, :, other_c, :, cols(h)], dst_ref=got.at[h],
            send_sem=sp.at[h], recv_sem=rp.at[h], device_id=(partner, my_t), device_id_type=MESH,
        ).start()

    def send_blocks(r):
        for i in range(nt):
            t = i // 2 if i % 2 == 0 else nt - 1 - i // 2

            def one(k, carry, t=t):
                dp = lax.rem(my_dp + k, nd)
                dst = dp * nt + t
                theirs, mine = pl.ds(dst * per, per), pl.ds(me * per, per)
                where = (dp, t)
                pltpu.make_async_remote_copy(
                    src_ref=xs_m.at[r, theirs], dst_ref=xr_m.at[r, mine],
                    send_sem=sm.at[r], recv_sem=rm.at[r], device_id=where, device_id_type=MESH,
                ).start()
                pltpu.make_async_remote_copy(
                    src_ref=xs_c.at[r, theirs], dst_ref=xr_c.at[r, mine],
                    send_sem=sc.at[r], recv_sem=rc.at[r], device_id=where, device_id_type=MESH,
                ).start()
                if r == 0:
                    pltpu.make_async_remote_copy(
                        src_ref=xs_s.at[theirs], dst_ref=xr_s.at[mine],
                        send_sem=ss.at[0], recv_sem=rs.at[0], device_id=where, device_id_type=MESH,
                    ).start()
                return carry

            lax.fori_loop(jnp.where(my_t == t, 1, 0), nd, one, 0)
        mine = pl.ds(me * per, per)
        pltpu.make_async_copy(xs_m.at[r, mine], xr_m.at[r, mine], rm.at[r]).start()
        pltpu.make_async_copy(xs_c.at[r, mine], xr_c.at[r, mine], rc.at[r]).start()
        if r == 0:
            pltpu.make_async_copy(xs_s.at[mine], xr_s.at[mine], rs.at[0]).start()

    def setup(h):
        k = h // 2
        if h % 2 == 0:
            return (keep_x.at[k], q1_x.at[k], r1_x.at[k], t1_x.at[k], u1_x.at[k],
                    q2_x.at[k], r2_x.at[k], t2_x.at[k], u2_x.at[k], my_y)
        return (keep_y.at[k], q1_y.at[k], r1_y.at[k], t1_y.at[k], u1_y.at[k],
                q2_y.at[k], r2_y.at[k], t2_y.at[k], u2_y.at[k], my_x)

    def at_first(h, a):
        return (my_y, other_x) if h % 2 == 0 else (row_away(a + 1), my_x)

    def at_second(h, b):
        return (row_away(b + 1), my_x) if h % 2 == 0 else (my_y, other_x)

    def slab(h, first, t):
        y, x = first
        return (t, x) if h % 2 == 0 else (y, t)

    def pair_sum(h, y, x):
        return own[y, x, :, cols(h)].astype(jnp.float32) + got[h, y, x].astype(jnp.float32)

    def pack(v, q, t):
        scale = scale_of(v)
        q[...] = jnp.round(v * (1.0 / scale)).astype(jnp.int16)
        t[:, :slots] = as_row(scale)

    def unpack(r, u):
        return r[...].astype(jnp.float32) * as_col(u[:, :slots])

    def remote(src, dst, send, recv, place):
        y, x = place
        pltpu.make_async_remote_copy(
            src_ref=src, dst_ref=dst, send_sem=send, recv_sem=recv,
            device_id=(dp_of(y, x, my_c), my_t), device_id_type=MESH,
        ).start()

    def first_stop(h):
        keep, q1, r1, t1, u1 = setup(h)[:5]
        with span(f"waitpair{h}"):
            drain(got.at[h], rp.at[h])
        for a in range(q1.shape[0]):
            place = at_first(h, a)
            for t in range(q1.shape[1]):
                pack(pair_sum(h, *slab(h, place, t)), q1.at[a, t], t1.at[a, t])
            remote(q1.at[a], r1.at[a], sa1.at[h], ra1.at[h], place)
            remote(t1.at[a], u1.at[a], sb1.at[h], rb1.at[h], place)
        for t in range(q1.shape[1]):
            keep[t] = pair_sum(h, *slab(h, (my_y, my_x), t))

    def second_stop(h):
        keep, q1, r1, t1, u1, q2, r2, t2, u2, mine = setup(h)
        with span(f"waitfirst{h}"):
            drain(r1, ra1.at[h])
            drain(u1, rb1.at[h])

        def total(t):
            return functools.reduce(jnp.add, [unpack(r1.at[a, t], u1.at[a, t]) for a in range(r1.shape[0])], keep[t])

        for b in range(q2.shape[0]):
            y, x = at_second(h, b)
            pack(total(y if h % 2 == 0 else x), q2.at[b], t2.at[b])
            remote(q2.at[b], r2.at[b], sa2.at[h], ra2.at[h], (y, x))
            remote(t2.at[b], u2.at[b], sb2.at[h], rb2.at[h], (y, x))
        keep[mine] = total(mine)

    with span("sendpairs"):
        for h in range(PARTS):
            send_pairs(h)
    with span("sendblocks0"):
        send_blocks(0)
    load_own.wait()
    for h in range(PARTS):
        with span(f"first{h}"):
            first_stop(h)
    with span("sendblocks1"):
        for r in range(1, RELAYS):
            send_blocks(r)
    for h in range(PARTS):
        with span(f"second{h}"):
            second_stop(h)

    inv_one = 1.0 / (1.0 - 0.9**STEP)
    inv_two = 1.0 / (1.0 - 0.95**STEP)

    def adam(h, s1, s2, s0, tops):
        if h * RELAYS % PARTS == 0:
            r = h * RELAYS // PARTS
            with span(f"waitblocks{r}"):
                drain(xr_m.at[r], rm.at[r])
                drain(xr_c.at[r], rc.at[r])
            xf_m[r] = xr_m[r].astype(jnp.float32).reshape(slots * cp, LANES)
            xf_c[r] = xr_c[r].astype(jnp.float32).reshape(slots * 2 * cp, LANES)
        keep, q1, r1, t1, u1, q2, r2, t2, u2, mine = setup(h)
        with span(f"waitsecond{h}"):
            drain(r2, ra2.at[h])
            drain(u2, rb2.at[h])
        top1, top2 = tops
        more = [as_col(u2[b, :, :slots]) for b in range(r2.shape[0])]
        for i in range(h * cq, (h + 1) * cq):
            at = slice(i * LANES, (i + 1) * LANES)
            r, j = i // cp, i % cp
            near = slice((i - h * cq) * LANES, (i - h * cq + 1) * LANES)
            grad = keep[mine, :, near]
            for b in range(r2.shape[0]):
                grad = grad + r2[b, :, near].astype(jnp.float32) * more[b]
            first = xf_c[r, pl.ds(j, slots, stride=2 * cp), :] * s1
            other = xf_c[r, pl.ds(cp + j, slots, stride=2 * cp), :] * s2
            old = xf_m[r, pl.ds(j, slots, stride=cp), :] * s0
            one = 0.9 * first + 0.1 * grad
            two = 0.95 * other + 0.05 * grad * grad
            update = (one * inv_one) / (jnp.sqrt(two * inv_two) + 1e-08) + 0.1 * old
            new = old - 0.01 * update
            nm_out[0, :, at] = new
            wg[0, my_dp, :, at] = new.astype(jnp.bfloat16)
            m1_v[:, at] = one
            m2_v[:, at] = two
            top1 = jnp.maximum(top1, jnp.abs(one))
            top2 = jnp.maximum(top2, jnp.abs(two))
        return top1, top2

    def gathered(chip, h):
        return wg.at[0, chip * 2 + my_c, :, cols(h)]

    def to_chip(h, chip, y, x):
        item = gathered(chip, h)
        pltpu.make_async_remote_copy(
            src_ref=item, dst_ref=item, send_sem=sa.at[h], recv_sem=ra.at[h, chip],
            device_id=(dp_of(y, x, my_c), my_t), device_id_type=MESH,
        ).start()

    def to_partner(h, chip):
        item = gathered(chip, h)
        pltpu.make_async_remote_copy(
            src_ref=item, dst_ref=item, send_sem=sf.at[h], recv_sem=rf.at[h],
            device_id=(partner, my_t), device_id_type=MESH,
        ).start()

    def arrived(h, chip):
        item = gathered(chip, h)
        pltpu.make_async_copy(item, item, ra.at[h, chip]).wait()

    rows_away = [row_away(away) for away in range(1, ny)]

    def spread(h):
        to_chip(h, my_chip, my_y, other_x)
        for y in rows_away:
            to_chip(h, my_chip, y, my_x)
        to_partner(h, my_chip)

    def relay(h):
        if h % 2 == 0:
            for y in rows_away:
                chip = y * 2 + my_x
                arrived(h, chip)
                to_chip(h, chip, my_y, other_x)
                to_partner(h, chip)
        else:
            chip = my_y * 2 + other_x
            arrived(h, chip)
            for y in rows_away:
                to_chip(h, chip, y, my_x)
            to_partner(h, chip)

    def finish(h):
        if h % 2 == 0:
            late = [my_y * 2 + other_x]
        else:
            late = [y * 2 + my_x for y in rows_away]
        for chip in late + [y * 2 + other_x for y in rows_away]:
            arrived(h, chip)
            to_partner(h, chip)

    with span("waitscales"):
        drain(xr_s, rs.at[0])
    scales = xr_s[:, 0, :]
    s1 = scales[:, 0:1]
    s2 = scales[:, LANES // 4:LANES // 4 + 1]
    s0 = scales[:, LANES // 2:LANES // 2 + 1]
    zero = jnp.zeros((slots, LANES), jnp.float32)
    tops = (zero, zero)
    for h in range(PARTS):
        with span(f"adam{h}"):
            tops = adam(h, s1, s2, s0, tops)
        with span(f"spread{h}"):
            spread(h)
        if h == PARTS // 2:
            for e in range(PARTS // 2):
                with span(f"relay{e}"):
                    relay(e)
    with span("relay2"):
        for h in range(PARTS // 2, PARTS - 1):
            relay(h)

    with span("codes"):
        top1 = jnp.max(tops[0], axis=1, keepdims=True) + 1e-06
        top2 = jnp.max(tops[1], axis=1, keepdims=True) + 1e-06
        ns1_out[...] = as_row(top1)
        ns2_out[...] = as_row(top2)
        inv1 = 1.0 / top1
        inv2 = 1.0 / top2
        for j in range(chunks):
            at = slice(j * LANES, (j + 1) * LANES)
            nc1_out[0, :, at] = (m1_v[:, at] * inv1).astype(jnp.bfloat16)
            nc2_out[0, :, at] = (m2_v[:, at] * inv2).astype(jnp.bfloat16)

    with span("relay3"):
        relay(PARTS - 1)
    with span("finish"):
        for h in range(PARTS):
            finish(h)
    with span("drainend"):
        for h in range(PARTS):
            keep, q1, r1, t1, u1, q2, r2, t2, u2, mine = setup(h)
            theirs = wg.at[0, pl.ds(0, chips), :, cols(h)]
            drain(theirs, rf.at[h])
            drain(theirs, sf.at[h])
            drain(wg.at[0, pl.ds(0, chips - 1), :, cols(h)], sa.at[h])
            drain(q1, sa1.at[h])
            drain(t1, sb1.at[h])
            drain(q2, sa2.at[h])
            drain(t2, sb2.at[h])
            drain(got.at[h], sp.at[h])
        for r in range(RELAYS):
            drain(xs_m.at[r, pl.ds(0, slots - per)], sm.at[r])
            drain(xs_c.at[r, pl.ds(0, slots - per)], sc.at[r])
        drain(xs_s.at[pl.ds(0, slots - per)], ss.at[0])


def _write_out(*refs):
    sem = refs[-1]
    count = (len(refs) - 1) // 2
    copies = [pltpu.make_async_copy(refs[i], refs[count + i], sem.at[i]) for i in range(count)]
    for item in copies:
        item.start()
    for item in copies:
        item.wait()


def _bytes(shape, dtype):
    return math.prod(shape) * jnp.dtype(dtype).itemsize


def on_device(send_order, master, first_code, first_scale, second_code, second_scale, grads):
    arrays = (send_order, master, first_code, first_scale, second_code, second_scale, grads)
    nd = lax.axis_size("dp")
    nt = lax.axis_size("tensor")
    slots = master.shape[1]
    width = master.shape[2]
    f32, b16, i16 = jnp.float32, jnp.bfloat16, jnp.int16
    dma = pltpu.SemaphoreType.DMA
    ny = nd // 4
    pairs = PARTS // 2
    wp = width // PARTS
    cp = width // LANES // RELAYS
    arrays = arrays[:6] + (grads.reshape(ny, 2, 2, slots, width),)
    results = (
        ((1, slots, width), f32),
        ((1, slots, width), b16),
        ((1, slots), f32),
        ((1, slots, width), b16),
        ((1, slots), f32),
        ((1, nd, slots, width), b16),
    )
    first_x, first_y = (pairs, 1, ny), (pairs, ny - 1, 2)
    then_x, then_y = (pairs, ny - 1), (pairs, 1)
    data = [(lead + (slots, wp), i16) for lead in (first_x, first_y, first_x, first_y, then_x, then_y, then_x, then_y)]
    sizes = [(lead + (1, LANES), f32) for lead in (first_x, first_y, first_x, first_y, then_x, then_y, then_x, then_y)]
    scratch = [
        ((1, slots), jnp.int32),
        ((1, slots), f32),
        ((1, slots), f32),
        ((slots, width), f32),
        ((slots, width), b16),
        ((slots, width), b16),
        ((RELAYS, slots * cp, LANES), f32),
        ((RELAYS, slots * 2 * cp, LANES), f32),
        ((RELAYS, slots, cp, LANES), i16),
        ((RELAYS, slots, 2 * cp, LANES), b16),
        ((slots, 1, LANES), f32),
        ((RELAYS, slots, cp, LANES), i16),
        ((RELAYS, slots, 2 * cp, LANES), b16),
        ((slots, 1, LANES), f32),
        ((ny, 2, slots, width), b16),
        ((PARTS, ny, 2, slots, wp), b16),
        ((pairs, ny, slots, wp), f32),
        ((pairs, 2, slots, wp), f32),
        *data,
        *sizes,
        ((slots, width), f32),
        ((slots, width), f32),
    ]
    grant = sum(_bytes(*item) for item in scratch) + sum(_bytes(*item) for item in results) + slots * 8192 + 6 * 1024 * 1024
    held = pl.pallas_call(
        functools.partial(_kernel, nd, nt, slots, width),
        out_shape=tuple(pltpu.VMEM(*item) for item in results),
        in_specs=[pl.BlockSpec(memory_space=pltpu.HBM)] * 7,
        out_specs=[pl.BlockSpec(memory_space=pltpu.VMEM)] * 6,
        scratch_shapes=[
            *(pltpu.VMEM(*item) for item in scratch),
            dma((6,)), dma((1,)),
            dma((RELAYS,)), dma((RELAYS,)), dma((1,)),
            dma((RELAYS,)), dma((RELAYS,)), dma((1,)),
            dma((PARTS,)), dma((PARTS,)),
            dma((PARTS,)), dma((PARTS,)), dma((PARTS,)), dma((PARTS,)),
            dma((PARTS,)), dma((PARTS,)), dma((PARTS,)), dma((PARTS,)),
            dma((PARTS, 2 * ny)), dma((PARTS,)), dma((PARTS,)), dma((PARTS,)),
        ],
        compiler_params=pltpu.CompilerParams(collective_id=0, has_side_effects=True, vmem_limit_bytes=grant),
        name="relayout_adam",
    )(*(pltpu.with_memory_space_constraint(item, pltpu.HBM) for item in arrays))
    return pl.pallas_call(
        _write_out,
        out_shape=tuple(jax.ShapeDtypeStruct(*item) for item in results),
        in_specs=[pl.BlockSpec(memory_space=pltpu.VMEM)] * len(results),
        out_specs=[pl.BlockSpec(memory_space=pltpu.HBM)] * len(results),
        scratch_shapes=[dma((len(results),))],
        compiler_params=pltpu.CompilerParams(vmem_limit_bytes=2 * 1024 * 1024),
        name="write_out",
    )(*(pltpu.with_memory_space_constraint(item, pltpu.VMEM) for item in held))


def solution(mesh):
    placed = (
        P(("dp", "tensor"), None),
        P(("dp", "tensor"), None, None),
        P(("dp", "tensor"), None, None),
        P(("dp", "tensor"), None),
        P(("dp", "tensor"), None, None),
        P(("dp", "tensor"), None),
        P("dp", "tensor", None, None, None),
    )
    return jax.shard_map(
        on_device,
        mesh=mesh,
        in_specs=placed,
        out_specs=(
            P(("dp", "tensor"), None, None),
            P(("dp", "tensor"), None, None),
            P(("dp", "tensor"), None),
            P(("dp", "tensor"), None, None),
            P(("dp", "tensor"), None),
            P("tensor", None, None, None),
        ),
        check_vma=False,
    )
```

```python
from contextlib import nullcontext as span
import functools
import math

import jax
import jax.numpy as jnp
from jax import lax
from jax.experimental import pallas as pl
from jax.experimental.pallas import tpu as pltpu
from jax.sharding import PartitionSpec as P

STEP = 10
LANES = 128
RELAYS = 2
PARTS = 4
LEVELS = 32767.0
TINY = 1e-30
MESH = pl.DeviceIdType.MESH


def _kernel(nd, nt, slots, width, order_hbm, m_hbm, c1_hbm, s1_hbm, c2_hbm, s2_hbm, g_hbm,
            nm_out, nc1_out, ns1_out, nc2_out, ns2_out, wg,
            order_v, s1_v, s2_v, m_v, c1_v, c2_v, xf_m, xf_c,
            xs_m, xs_c, xs_s, xr_m, xr_c, xr_s, own, got,
            keep_x, keep_y, q1_x, q1_y, r1_x, r1_y, q2_x, q2_y, r2_x, r2_y,
            t1_x, t1_y, u1_x, u1_y, t2_x, t2_y, u2_x, u2_y, m1_v, m2_v,
            in_sem, own_sem, rm, rc, rs, sm, sc, ss, rp, sp,
            ra1, sa1, rb1, sb1, ra2, sa2, rb2, sb2, ra, sa, rf, sf, plane_in):
    n = nd * nt
    per = slots // n
    chunks = width // LANES
    cp = chunks // RELAYS
    cq = chunks // PARTS
    wr = width // RELAYS
    wp = width // PARTS
    ny = nd // 4
    chips = 2 * ny
    my_dp = lax.axis_index("dp")
    my_t = lax.axis_index("tensor")
    me = my_dp * nt + my_t
    my_c = lax.rem(my_dp, 2)
    my_chip = my_dp // 2
    my_x = lax.rem(my_chip, 2)
    my_y = my_chip // 2
    other_c = 1 - my_c
    other_x = 1 - my_x
    partner = my_dp + 1 - 2 * my_c

    def dp_of(y, x, c):
        return (y * 2 + x) * 2 + c

    def row_away(away):
        return lax.rem(my_y + away, ny)

    barrier = pltpu.get_barrier_semaphore()

    def greet_column(k, carry):
        pl.semaphore_signal(barrier, inc=1, device_id=(my_dp, lax.rem(my_t + k, nt)), device_id_type=MESH)
        return carry

    def greet_plane(k, carry):
        pl.semaphore_signal(barrier, inc=1, device_id=(lax.rem(my_dp + k, nd), my_t), device_id_type=MESH)
        return carry

    lax.fori_loop(1, nt, greet_column, 0)
    lax.fori_loop(1, nd, greet_plane, 0)

    loads = [
        pltpu.make_async_copy(order_hbm, order_v, in_sem.at[0]),
        pltpu.make_async_copy(m_hbm.at[0], m_v, in_sem.at[3]),
        pltpu.make_async_copy(s1_hbm, s1_v, in_sem.at[1]),
        pltpu.make_async_copy(s2_hbm, s2_v, in_sem.at[2]),
        pltpu.make_async_copy(c1_hbm.at[0], c1_v, in_sem.at[4]),
        pltpu.make_async_copy(c2_hbm.at[0], c2_v, in_sem.at[5]),
    ]
    for item in loads:
        item.start()

    def cols(h):
        return pl.ds(h * wp, wp)

    def wide(r):
        return pl.ds(r * wr, wr)

    def drain(ref, sem):
        pltpu.make_async_copy(ref, ref, sem).wait()

    with span("loads"):
        for item in loads:
            item.wait()
    load_own = pltpu.make_async_copy(g_hbm.at[:, :, my_c], own, own_sem.at[0])
    load_own.start()

    eye = lax.broadcasted_iota(jnp.int32, (slots, slots), 0) == lax.broadcasted_iota(jnp.int32, (slots, slots), 1)

    def as_row(col):
        return jnp.sum(jnp.where(eye, col, 0.0), axis=0, keepdims=True)

    def as_col(row):
        return jnp.sum(jnp.where(eye, row, 0.0), axis=1, keepdims=True)

    def scale_of(x):
        return (jnp.max(jnp.abs(x), axis=1, keepdims=True) + TINY) * (1.0 / LEVELS)

    with span("prep"):
        lane = lax.broadcasted_iota(jnp.int32, (slots, slots), 1)
        order_col = as_col(order_v[...].astype(jnp.float32))
        pick = order_col == lane.astype(jnp.float32)

        def picked(row):
            return jnp.sum(jnp.where(pick, row, 0.0), axis=1, keepdims=True)

        m_scale = scale_of(m_v[...])
        m_inv = 1.0 / m_scale
        place = lax.broadcasted_iota(jnp.int32, (slots, LANES), 1)
        both = jnp.where(place < LANES // 4, picked(s1_v[...]), picked(s2_v[...]))
        xs_s[:, 0, :] = jnp.where(place < LANES // 2, both, picked(as_row(m_scale)))
        select = jnp.where(pick, 1.0, 0.0).astype(jnp.bfloat16)

    def take(x):
        return jnp.dot(select, x, preferred_element_type=jnp.float32)

    def stage(r):
        level = jnp.round(m_v[:, wide(r)] * m_inv)
        high = jnp.round(level * (1.0 / 256.0))
        low = level - 256.0 * high
        xm = 256.0 * take(high.astype(jnp.bfloat16)) + take(low.astype(jnp.bfloat16))
        x1 = take(c1_v[:, wide(r)])
        x2 = take(c2_v[:, wide(r)])
        for j in range(cp):
            piece = slice(j * LANES, (j + 1) * LANES)
            xf_m[r, pl.ds(j, slots, stride=cp), :] = xm[:, piece]
            xf_c[r, pl.ds(j, slots, stride=2 * cp), :] = x1[:, piece]
            xf_c[r, pl.ds(cp + j, slots, stride=2 * cp), :] = x2[:, piece]
        xs_m[r] = xf_m[r].reshape(slots, cp, LANES).astype(jnp.int16)
        xs_c[r] = xf_c[r].reshape(slots, 2 * cp, LANES).astype(jnp.bfloat16)

    with span("stage"):
        for r in range(RELAYS):
            stage(r)

    with span("barrier"):
        pl.semaphore_wait(barrier, nd - 1 + nt - 1)

    def announce(k, carry):
        pl.semaphore_signal(plane_in.at[my_t], inc=1, device_id=(my_dp, lax.rem(my_t + k, nt)), device_id_type=MESH)
        return carry

    lax.fori_loop(1, nt, announce, 0)

    def send_pairs(h):
        pltpu.make_async_remote_copy(
            src_ref=g_hbm.at[:, :, other_c, :, cols(h)], dst_ref=got.at[h],
            send_sem=sp.at[h], recv_sem=rp.at[h], device_id=(partner, my_t), device_id_type=MESH,
        ).start()

    def send_blocks(r):
        for t in range(nt):
            if r == 0:
                @pl.when(my_t != t)
                def _(t=t):
                    pl.semaphore_wait(plane_in.at[t], 1)

            def one(k, carry, t=t):
                dp = lax.rem(my_dp + k, nd)
                dst = dp * nt + t
                theirs, mine = pl.ds(dst * per, per), pl.ds(me * per, per)
                where = (dp, t)
                pltpu.make_async_remote_copy(
                    src_ref=xs_m.at[r, theirs], dst_ref=xr_m.at[r, mine],
                    send_sem=sm.at[r], recv_sem=rm.at[r], device_id=where, device_id_type=MESH,
                ).start()
                pltpu.make_async_remote_copy(
                    src_ref=xs_c.at[r, theirs], dst_ref=xr_c.at[r, mine],
                    send_sem=sc.at[r], recv_sem=rc.at[r], device_id=where, device_id_type=MESH,
                ).start()
                if r == 0:
                    pltpu.make_async_remote_copy(
                        src_ref=xs_s.at[theirs], dst_ref=xr_s.at[mine],
                        send_sem=ss.at[0], recv_sem=rs.at[0], device_id=where, device_id_type=MESH,
                    ).start()
                return carry

            lax.fori_loop(jnp.where(my_t == t, 1, 0), nd, one, 0)
        mine = pl.ds(me * per, per)
        pltpu.make_async_copy(xs_m.at[r, mine], xr_m.at[r, mine], rm.at[r]).start()
        pltpu.make_async_copy(xs_c.at[r, mine], xr_c.at[r, mine], rc.at[r]).start()
        if r == 0:
            pltpu.make_async_copy(xs_s.at[mine], xr_s.at[mine], rs.at[0]).start()

    def setup(h):
        k = h // 2
        if h % 2 == 0:
            return (keep_x.at[k], q1_x.at[k], r1_x.at[k], t1_x.at[k], u1_x.at[k],
                    q2_x.at[k], r2_x.at[k], t2_x.at[k], u2_x.at[k], my_y)
        return (keep_y.at[k], q1_y.at[k], r1_y.at[k], t1_y.at[k], u1_y.at[k],
                q2_y.at[k], r2_y.at[k], t2_y.at[k], u2_y.at[k], my_x)

    def at_first(h, a):
        return (my_y, other_x) if h % 2 == 0 else (row_away(a + 1), my_x)

    def at_second(h, b):
        return (row_away(b + 1), my_x) if h % 2 == 0 else (my_y, other_x)

    def slab(h, first, t):
        y, x = first
        return (t, x) if h % 2 == 0 else (y, t)

    def pair_sum(h, y, x):
        return own[y, x, :, cols(h)].astype(jnp.float32) + got[h, y, x].astype(jnp.float32)

    def pack(v, q, t):
        scale = scale_of(v)
        q[...] = jnp.round(v * (1.0 / scale)).astype(jnp.int16)
        t[:, :slots] = as_row(scale)

    def unpack(r, u):
        return r[...].astype(jnp.float32) * as_col(u[:, :slots])

    def remote(src, dst, send, recv, place):
        y, x = place
        pltpu.make_async_remote_copy(
            src_ref=src, dst_ref=dst, send_sem=send, recv_sem=recv,
            device_id=(dp_of(y, x, my_c), my_t), device_id_type=MESH,
        ).start()

    def first_stop(h):
        keep, q1, r1, t1, u1 = setup(h)[:5]
        with span(f"waitpair{h}"):
            drain(got.at[h], rp.at[h])
        for a in range(q1.shape[0]):
            place = at_first(h, a)
            for t in range(q1.shape[1]):
                pack(pair_sum(h, *slab(h, place, t)), q1.at[a, t], t1.at[a, t])
            remote(q1.at[a], r1.at[a], sa1.at[h], ra1.at[h], place)
            remote(t1.at[a], u1.at[a], sb1.at[h], rb1.at[h], place)
        for t in range(q1.shape[1]):
            keep[t] = pair_sum(h, *slab(h, (my_y, my_x), t))

    def second_stop(h):
        keep, q1, r1, t1, u1, q2, r2, t2, u2, mine = setup(h)
        with span(f"waitfirst{h}"):
            drain(r1, ra1.at[h])
            drain(u1, rb1.at[h])

        def total(t):
            return functools.reduce(jnp.add, [unpack(r1.at[a, t], u1.at[a, t]) for a in range(r1.shape[0])], keep[t])

        for b in range(q2.shape[0]):
            y, x = at_second(h, b)
            pack(total(y if h % 2 == 0 else x), q2.at[b], t2.at[b])
            remote(q2.at[b], r2.at[b], sa2.at[h], ra2.at[h], (y, x))
            remote(t2.at[b], u2.at[b], sb2.at[h], rb2.at[h], (y, x))
        keep[mine] = total(mine)

    with span("sendpairs"):
        for h in range(PARTS):
            send_pairs(h)
    load_own.wait()

    def first_stops():
        for h in range(PARTS):
            with span(f"first{h}"):
                first_stop(h)

    pl.when(2 * my_t < nt)(first_stops)
    with span("sendblocks0"):
        send_blocks(0)
    pl.when(2 * my_t >= nt)(first_stops)
    with span("sendblocks1"):
        for r in range(1, RELAYS):
            send_blocks(r)
    for h in range(PARTS):
        with span(f"second{h}"):
            second_stop(h)

    inv_one = 1.0 / (1.0 - 0.9**STEP)
    inv_two = 1.0 / (1.0 - 0.95**STEP)

    def adam(h, s1, s2, s0, tops):
        if h * RELAYS % PARTS == 0:
            r = h * RELAYS // PARTS
            with span(f"waitblocks{r}"):
                drain(xr_m.at[r], rm.at[r])
                drain(xr_c.at[r], rc.at[r])
            xf_m[r] = xr_m[r].astype(jnp.float32).reshape(slots * cp, LANES)
            xf_c[r] = xr_c[r].astype(jnp.float32).reshape(slots * 2 * cp, LANES)
        keep, q1, r1, t1, u1, q2, r2, t2, u2, mine = setup(h)
        with span(f"waitsecond{h}"):
            drain(r2, ra2.at[h])
            drain(u2, rb2.at[h])
        top1, top2 = tops
        more = [as_col(u2[b, :, :slots]) for b in range(r2.shape[0])]
        for i in range(h * cq, (h + 1) * cq):
            at = slice(i * LANES, (i + 1) * LANES)
            r, j = i // cp, i % cp
            near = slice((i - h * cq) * LANES, (i - h * cq + 1) * LANES)
            grad = keep[mine, :, near]
            for b in range(r2.shape[0]):
                grad = grad + r2[b, :, near].astype(jnp.float32) * more[b]
            first = xf_c[r, pl.ds(j, slots, stride=2 * cp), :] * s1
            other = xf_c[r, pl.ds(cp + j, slots, stride=2 * cp), :] * s2
            old = xf_m[r, pl.ds(j, slots, stride=cp), :] * s0
            one = 0.9 * first + 0.1 * grad
            two = 0.95 * other + 0.05 * grad * grad
            update = (one * inv_one) / (jnp.sqrt(two * inv_two) + 1e-08) + 0.1 * old
            new = old - 0.01 * update
            nm_out[0, :, at] = new
            wg[0, my_dp, :, at] = new.astype(jnp.bfloat16)
            m1_v[:, at] = one
            m2_v[:, at] = two
            top1 = jnp.maximum(top1, jnp.abs(one))
            top2 = jnp.maximum(top2, jnp.abs(two))
        return top1, top2

    def gathered(chip, h):
        return wg.at[0, chip * 2 + my_c, :, cols(h)]

    def to_chip(h, chip, y, x):
        item = gathered(chip, h)
        pltpu.make_async_remote_copy(
            src_ref=item, dst_ref=item, send_sem=sa.at[h], recv_sem=ra.at[h, chip],
            device_id=(dp_of(y, x, my_c), my_t), device_id_type=MESH,
        ).start()

    def to_partner(h, chip):
        item = gathered(chip, h)
        pltpu.make_async_remote_copy(
            src_ref=item, dst_ref=item, send_sem=sf.at[h], recv_sem=rf.at[h],
            device_id=(partner, my_t), device_id_type=MESH,
        ).start()

    def arrived(h, chip):
        item = gathered(chip, h)
        pltpu.make_async_copy(item, item, ra.at[h, chip]).wait()

    rows_away = [row_away(away) for away in range(1, ny)]

    def spread(h):
        to_chip(h, my_chip, my_y, other_x)
        for y in rows_away:
            to_chip(h, my_chip, y, my_x)
        to_partner(h, my_chip)

    def relay(h):
        if h % 2 == 0:
            for y in rows_away:
                chip = y * 2 + my_x
                arrived(h, chip)
                to_chip(h, chip, my_y, other_x)
                to_partner(h, chip)
        else:
            chip = my_y * 2 + other_x
            arrived(h, chip)
            for y in rows_away:
                to_chip(h, chip, y, my_x)
            to_partner(h, chip)

    def finish(h):
        if h % 2 == 0:
            late = [my_y * 2 + other_x]
        else:
            late = [y * 2 + my_x for y in rows_away]
        for chip in late + [y * 2 + other_x for y in rows_away]:
            arrived(h, chip)
            to_partner(h, chip)

    with span("waitscales"):
        drain(xr_s, rs.at[0])
    scales = xr_s[:, 0, :]
    s1 = scales[:, 0:1]
    s2 = scales[:, LANES // 4:LANES // 4 + 1]
    s0 = scales[:, LANES // 2:LANES // 2 + 1]
    zero = jnp.zeros((slots, LANES), jnp.float32)
    tops = (zero, zero)
    for h in range(PARTS):
        with span(f"adam{h}"):
            tops = adam(h, s1, s2, s0, tops)
        with span(f"spread{h}"):
            spread(h)
        if h == PARTS // 2 - 1:
            for e in range(PARTS // 2):
                with span(f"relay{e}"):
                    relay(e)
    with span("relay2"):
        for h in range(PARTS // 2, PARTS - 1):
            relay(h)

    with span("codes"):
        top1 = jnp.max(tops[0], axis=1, keepdims=True) + 1e-06
        top2 = jnp.max(tops[1], axis=1, keepdims=True) + 1e-06
        ns1_out[...] = as_row(top1)
        ns2_out[...] = as_row(top2)
        inv1 = 1.0 / top1
        inv2 = 1.0 / top2
        for j in range(chunks):
            at = slice(j * LANES, (j + 1) * LANES)
            nc1_out[0, :, at] = (m1_v[:, at] * inv1).astype(jnp.bfloat16)
            nc2_out[0, :, at] = (m2_v[:, at] * inv2).astype(jnp.bfloat16)

    with span("relay3"):
        relay(PARTS - 1)
    with span("finish"):
        for h in range(PARTS):
            finish(h)
    with span("drainend"):
        for h in range(PARTS):
            keep, q1, r1, t1, u1, q2, r2, t2, u2, mine = setup(h)
            theirs = wg.at[0, pl.ds(0, chips), :, cols(h)]
            drain(theirs, rf.at[h])
            drain(theirs, sf.at[h])
            drain(wg.at[0, pl.ds(0, chips - 1), :, cols(h)], sa.at[h])
            drain(q1, sa1.at[h])
            drain(t1, sb1.at[h])
            drain(q2, sa2.at[h])
            drain(t2, sb2.at[h])
            drain(got.at[h], sp.at[h])
        for r in range(RELAYS):
            drain(xs_m.at[r, pl.ds(0, slots - per)], sm.at[r])
            drain(xs_c.at[r, pl.ds(0, slots - per)], sc.at[r])
        drain(xs_s.at[pl.ds(0, slots - per)], ss.at[0])


def _write_out(*refs):
    sem = refs[-1]
    count = (len(refs) - 1) // 2
    copies = [pltpu.make_async_copy(refs[i], refs[count + i], sem.at[i]) for i in range(count)]
    for item in copies:
        item.start()
    for item in copies:
        item.wait()


def _bytes(shape, dtype):
    return math.prod(shape) * jnp.dtype(dtype).itemsize


def on_device(send_order, master, first_code, first_scale, second_code, second_scale, grads):
    arrays = (send_order, master, first_code, first_scale, second_code, second_scale, grads)
    nd = lax.axis_size("dp")
    nt = lax.axis_size("tensor")
    slots = master.shape[1]
    width = master.shape[2]
    f32, b16, i16 = jnp.float32, jnp.bfloat16, jnp.int16
    dma = pltpu.SemaphoreType.DMA
    ny = nd // 4
    pairs = PARTS // 2
    wp = width // PARTS
    cp = width // LANES // RELAYS
    arrays = arrays[:6] + (grads.reshape(ny, 2, 2, slots, width),)
    results = (
        ((1, slots, width), f32),
        ((1, slots, width), b16),
        ((1, slots), f32),
        ((1, slots, width), b16),
        ((1, slots), f32),
        ((1, nd, slots, width), b16),
    )
    first_x, first_y = (pairs, 1, ny), (pairs, ny - 1, 2)
    then_x, then_y = (pairs, ny - 1), (pairs, 1)
    data = [(lead + (slots, wp), i16) for lead in (first_x, first_y, first_x, first_y, then_x, then_y, then_x, then_y)]
    sizes = [(lead + (1, LANES), f32) for lead in (first_x, first_y, first_x, first_y, then_x, then_y, then_x, then_y)]
    scratch = [
        ((1, slots), jnp.int32),
        ((1, slots), f32),
        ((1, slots), f32),
        ((slots, width), f32),
        ((slots, width), b16),
        ((slots, width), b16),
        ((RELAYS, slots * cp, LANES), f32),
        ((RELAYS, slots * 2 * cp, LANES), f32),
        ((RELAYS, slots, cp, LANES), i16),
        ((RELAYS, slots, 2 * cp, LANES), b16),
        ((slots, 1, LANES), f32),
        ((RELAYS, slots, cp, LANES), i16),
        ((RELAYS, slots, 2 * cp, LANES), b16),
        ((slots, 1, LANES), f32),
        ((ny, 2, slots, width), b16),
        ((PARTS, ny, 2, slots, wp), b16),
        ((pairs, ny, slots, wp), f32),
        ((pairs, 2, slots, wp), f32),
        *data,
        *sizes,
        ((slots, width), f32),
        ((slots, width), f32),
    ]
    grant = sum(_bytes(*item) for item in scratch) + sum(_bytes(*item) for item in results) + slots * 8192 + 6 * 1024 * 1024
    held = pl.pallas_call(
        functools.partial(_kernel, nd, nt, slots, width),
        out_shape=tuple(pltpu.VMEM(*item) for item in results),
        in_specs=[pl.BlockSpec(memory_space=pltpu.HBM)] * 7,
        out_specs=[pl.BlockSpec(memory_space=pltpu.VMEM)] * 6,
        scratch_shapes=[
            *(pltpu.VMEM(*item) for item in scratch),
            dma((6,)), dma((1,)),
            dma((RELAYS,)), dma((RELAYS,)), dma((1,)),
            dma((RELAYS,)), dma((RELAYS,)), dma((1,)),
            dma((PARTS,)), dma((PARTS,)),
            dma((PARTS,)), dma((PARTS,)), dma((PARTS,)), dma((PARTS,)),
            dma((PARTS,)), dma((PARTS,)), dma((PARTS,)), dma((PARTS,)),
            dma((PARTS, 2 * ny)), dma((PARTS,)), dma((PARTS,)), dma((PARTS,)),
            pltpu.SemaphoreType.REGULAR((nt,)),
        ],
        compiler_params=pltpu.CompilerParams(collective_id=0, has_side_effects=True, vmem_limit_bytes=grant),
        name="relayout_adam",
    )(*(pltpu.with_memory_space_constraint(item, pltpu.HBM) for item in arrays))
    return pl.pallas_call(
        _write_out,
        out_shape=tuple(jax.ShapeDtypeStruct(*item) for item in results),
        in_specs=[pl.BlockSpec(memory_space=pltpu.VMEM)] * len(results),
        out_specs=[pl.BlockSpec(memory_space=pltpu.HBM)] * len(results),
        scratch_shapes=[dma((len(results),))],
        compiler_params=pltpu.CompilerParams(vmem_limit_bytes=2 * 1024 * 1024),
        name="write_out",
    )(*(pltpu.with_memory_space_constraint(item, pltpu.VMEM) for item in held))


def solution(mesh):
    placed = (
        P(("dp", "tensor"), None),
        P(("dp", "tensor"), None, None),
        P(("dp", "tensor"), None, None),
        P(("dp", "tensor"), None),
        P(("dp", "tensor"), None, None),
        P(("dp", "tensor"), None),
        P("dp", "tensor", None, None, None),
    )
    return jax.shard_map(
        on_device,
        mesh=mesh,
        in_specs=placed,
        out_specs=(
            P(("dp", "tensor"), None, None),
            P(("dp", "tensor"), None, None),
            P(("dp", "tensor"), None),
            P(("dp", "tensor"), None, None),
            P(("dp", "tensor"), None),
            P("tensor", None, None, None),
        ),
        check_vma=False,
    )
```

```python
from contextlib import nullcontext as span
import functools
import math

import jax
import jax.numpy as jnp
from jax import lax
from jax.experimental import pallas as pl
from jax.experimental.pallas import tpu as pltpu
from jax.sharding import PartitionSpec as P

STEP = 10
LANES = 128
RELAYS = 2
PARTS = 4
LEVELS = 32767.0
TINY = 1e-30
MESH = pl.DeviceIdType.MESH


def _kernel(nd, nt, slots, width, order_hbm, m_hbm, c1_hbm, s1_hbm, c2_hbm, s2_hbm, g_hbm,
            nm_out, nc1_out, ns1_out, nc2_out, ns2_out, wg,
            order_v, s1_v, s2_v, m_v, c1_v, c2_v, xf_m, xf_c,
            xs_m, xs_c, xs_s, xr_m, xr_c, xr_s, own, got,
            keep_x, keep_y, q1_x, q1_y, r1_x, r1_y, q2_x, q2_y, r2_x, r2_y,
            t1_x, t1_y, u1_x, u1_y, t2_x, t2_y, u2_x, u2_y, m1_v, m2_v,
            in_sem, own_sem, sent, rm, rc, rs, rp, r1st, u1st, r2nd, u2nd, ra, rf, plane_in):
    n = nd * nt
    per = slots // n
    chunks = width // LANES
    cp = chunks // RELAYS
    cq = chunks // PARTS
    wr = width // RELAYS
    wp = width // PARTS
    ny = nd // 4
    chips = 2 * ny
    my_dp = lax.axis_index("dp")
    my_t = lax.axis_index("tensor")
    me = my_dp * nt + my_t
    my_c = lax.rem(my_dp, 2)
    my_chip = my_dp // 2
    my_x = lax.rem(my_chip, 2)
    my_y = my_chip // 2
    other_c = 1 - my_c
    other_x = 1 - my_x
    partner = my_dp + 1 - 2 * my_c

    def dp_of(y, x, c):
        return (y * 2 + x) * 2 + c

    def row_away(away):
        return lax.rem(my_y + away, ny)

    barrier = pltpu.get_barrier_semaphore()

    def tell(sem, up):
        where = (my_dp, my_t + 1 if up else my_t - 1)

        @pl.when(my_t < nt - 1 if up else my_t > 0)
        def _():
            pl.semaphore_signal(sem, inc=1, device_id=where, device_id_type=MESH)

    def greet(k, carry):
        pl.semaphore_signal(barrier, inc=1, device_id=(lax.rem(my_dp + k, nd), my_t), device_id_type=MESH)
        return carry

    tell(barrier, True)
    tell(barrier, False)
    lax.fori_loop(1, nd, greet, 0)

    loads = [
        pltpu.make_async_copy(order_hbm, order_v, in_sem.at[0]),
        pltpu.make_async_copy(m_hbm.at[0], m_v, in_sem.at[3]),
        pltpu.make_async_copy(s1_hbm, s1_v, in_sem.at[1]),
        pltpu.make_async_copy(s2_hbm, s2_v, in_sem.at[2]),
        pltpu.make_async_copy(c1_hbm.at[0], c1_v, in_sem.at[4]),
        pltpu.make_async_copy(c2_hbm.at[0], c2_v, in_sem.at[5]),
    ]
    for item in loads:
        item.start()

    def cols(h):
        return pl.ds(h * wp, wp)

    def wide(r):
        return pl.ds(r * wr, wr)

    def drain(ref, sem):
        pltpu.make_async_copy(ref, ref, sem).wait()

    load_own = pltpu.make_async_copy(g_hbm.at[:, :, my_c], own, own_sem.at[0])

    def send_pairs(h):
        pltpu.make_async_remote_copy(
            src_ref=g_hbm.at[:, :, other_c, :, cols(h)], dst_ref=got.at[h],
            send_sem=sent.at[0], recv_sem=rp.at[h], device_id=(partner, my_t), device_id_type=MESH,
        ).start()

    with span("barrier"):
        beside_me = jnp.where(my_t > 0, 1, 0) + jnp.where(my_t < nt - 1, 1, 0)
        pl.semaphore_wait(barrier, nd - 1 + beside_me)

    tell(plane_in.at[my_t], True)
    tell(plane_in.at[my_t], False)
    for h in range(PARTS):
        send_pairs(h)
    load_own.start()

    with span("loads"):
        for item in loads:
            item.wait()

    eye = lax.broadcasted_iota(jnp.int32, (slots, slots), 0) == lax.broadcasted_iota(jnp.int32, (slots, slots), 1)

    def as_row(col):
        return jnp.sum(jnp.where(eye, col, 0.0), axis=0, keepdims=True)

    def as_col(row):
        return jnp.sum(jnp.where(eye, row, 0.0), axis=1, keepdims=True)

    def scale_of(x):
        return (jnp.max(jnp.abs(x), axis=1, keepdims=True) + TINY) * (1.0 / LEVELS)

    with span("prep"):
        lane = lax.broadcasted_iota(jnp.int32, (slots, slots), 1)
        order_col = as_col(order_v[...].astype(jnp.float32))
        pick = order_col == lane.astype(jnp.float32)

        def picked(row):
            return jnp.sum(jnp.where(pick, row, 0.0), axis=1, keepdims=True)

        m_scale = scale_of(m_v[...])
        m_inv = 1.0 / m_scale
        place = lax.broadcasted_iota(jnp.int32, (slots, LANES), 1)
        both = jnp.where(place < LANES // 4, picked(s1_v[...]), picked(s2_v[...]))
        xs_s[:, 0, :] = jnp.where(place < LANES // 2, both, picked(as_row(m_scale)))
        select = jnp.where(pick, 1.0, 0.0).astype(jnp.bfloat16)

    def take(x):
        return jnp.dot(select, x, preferred_element_type=jnp.float32)

    def stage(r):
        level = jnp.round(m_v[:, wide(r)] * m_inv)
        high = jnp.round(level * (1.0 / 256.0))
        low = level - 256.0 * high
        xm = 256.0 * take(high.astype(jnp.bfloat16)) + take(low.astype(jnp.bfloat16))
        x1 = take(c1_v[:, wide(r)])
        x2 = take(c2_v[:, wide(r)])
        for j in range(cp):
            piece = slice(j * LANES, (j + 1) * LANES)
            xf_m[r, pl.ds(j, slots, stride=cp), :] = xm[:, piece]
            xf_c[r, pl.ds(j, slots, stride=2 * cp), :] = x1[:, piece]
            xf_c[r, pl.ds(cp + j, slots, stride=2 * cp), :] = x2[:, piece]
        xs_m[r] = xf_m[r].reshape(slots, cp, LANES).astype(jnp.int16)
        xs_c[r] = xf_c[r].reshape(slots, 2 * cp, LANES).astype(jnp.bfloat16)

    with span("stage"):
        for r in range(RELAYS):
            stage(r)

    def send_block(r, t, dp):
        dst = dp * nt + t
        theirs, mine = pl.ds(dst * per, per), pl.ds(me * per, per)
        where = (dp, t)
        pltpu.make_async_remote_copy(
            src_ref=xs_m.at[r, theirs], dst_ref=xr_m.at[r, mine],
            send_sem=sent.at[9], recv_sem=rm.at[r], device_id=where, device_id_type=MESH,
        ).start()
        pltpu.make_async_remote_copy(
            src_ref=xs_c.at[r, theirs], dst_ref=xr_c.at[r, mine],
            send_sem=sent.at[10], recv_sem=rc.at[r], device_id=where, device_id_type=MESH,
        ).start()
        if r == 0:
            pltpu.make_async_remote_copy(
                src_ref=xs_s.at[theirs], dst_ref=xr_s.at[mine],
                send_sem=sent.at[11], recv_sem=rs.at[0], device_id=where, device_id_type=MESH,
            ).start()

    early = 2 * my_t < nt

    def send_blocks():
        for i in range(nt):
            t = jnp.where(early, i, lax.rem(nt - i, nt))

            @pl.when(my_t != t)
            def _(t=t):
                pl.semaphore_wait(plane_in.at[t], 1)

            pl.when(t < my_t)(functools.partial(tell, plane_in.at[t], True))
            pl.when(t > my_t)(functools.partial(tell, plane_in.at[t], False))

            for r in range(RELAYS):
                def one(k, carry, r=r, t=t):
                    send_block(r, t, lax.rem(my_dp + k, nd))
                    return carry

                lax.fori_loop(jnp.where(my_t == t, 1, 0), nd, one, 0)
        mine = pl.ds(me * per, per)
        pltpu.make_async_copy(xs_s.at[mine], xr_s.at[mine], rs.at[0]).start()
        for r in range(RELAYS):
            pltpu.make_async_copy(xs_m.at[r, mine], xr_m.at[r, mine], rm.at[r]).start()
            pltpu.make_async_copy(xs_c.at[r, mine], xr_c.at[r, mine], rc.at[r]).start()

    def setup(h):
        k = h // 2
        if h % 2 == 0:
            return (keep_x.at[k], q1_x.at[k], r1_x.at[k], t1_x.at[k], u1_x.at[k],
                    q2_x.at[k], r2_x.at[k], t2_x.at[k], u2_x.at[k], my_y)
        return (keep_y.at[k], q1_y.at[k], r1_y.at[k], t1_y.at[k], u1_y.at[k],
                q2_y.at[k], r2_y.at[k], t2_y.at[k], u2_y.at[k], my_x)

    def at_first(h, a):
        return (my_y, other_x) if h % 2 == 0 else (row_away(a + 1), my_x)

    def at_second(h, b):
        return (row_away(b + 1), my_x) if h % 2 == 0 else (my_y, other_x)

    def slab(h, first, t):
        y, x = first
        return (t, x) if h % 2 == 0 else (y, t)

    def pair_sum(h, y, x):
        return own[y, x, :, cols(h)].astype(jnp.float32) + got[h, y, x].astype(jnp.float32)

    def pack(v, q, t):
        scale = scale_of(v)
        q[...] = jnp.round(v * (1.0 / scale)).astype(jnp.int16)
        t[:, :slots] = as_row(scale)

    def unpack(r, u):
        return r[...].astype(jnp.float32) * as_col(u[:, :slots])

    def remote(src, dst, send, recv, place):
        y, x = place
        pltpu.make_async_remote_copy(
            src_ref=src, dst_ref=dst, send_sem=sent.at[send], recv_sem=recv,
            device_id=(dp_of(y, x, my_c), my_t), device_id_type=MESH,
        ).start()

    def first_stop(h):
        keep, q1, r1, t1, u1 = setup(h)[:5]
        with span(f"waitpair{h}"):
            drain(got.at[h], rp.at[h])
        for a in range(q1.shape[0]):
            place = at_first(h, a)
            for t in range(q1.shape[1]):
                pack(pair_sum(h, *slab(h, place, t)), q1.at[a, t], t1.at[a, t])
            remote(q1.at[a], r1.at[a], 1 + h % 2, r1st.at[h], place)
            remote(t1.at[a], u1.at[a], 3 + h % 2, u1st.at[h], place)
        for t in range(q1.shape[1]):
            keep[t] = pair_sum(h, *slab(h, (my_y, my_x), t))

    def second_stop(h):
        keep, q1, r1, t1, u1, q2, r2, t2, u2, mine = setup(h)
        with span(f"waitfirst{h}"):
            drain(r1, r1st.at[h])
            drain(u1, u1st.at[h])

        def total(t):
            return functools.reduce(jnp.add, [unpack(r1.at[a, t], u1.at[a, t]) for a in range(r1.shape[0])], keep[t])

        for b in range(q2.shape[0]):
            y, x = at_second(h, b)
            pack(total(y if h % 2 == 0 else x), q2.at[b], t2.at[b])
            remote(q2.at[b], r2.at[b], 5 + h % 2, r2nd.at[h], (y, x))
            remote(t2.at[b], u2.at[b], 7 + h % 2, u2nd.at[h], (y, x))
        keep[mine] = total(mine)

    def first_stops():
        load_own.wait()
        for h in range(PARTS):
            with span(f"first{h}"):
                first_stop(h)

    pl.when(early)(first_stops)
    with span("sendblocks0"):
        send_blocks()
    pl.when(jnp.logical_not(early))(first_stops)
    for h in range(PARTS):
        with span(f"second{h}"):
            second_stop(h)

    inv_one = 1.0 / (1.0 - 0.9**STEP)
    inv_two = 1.0 / (1.0 - 0.95**STEP)

    def adam(h, tops):
        if h * RELAYS % PARTS == 0:
            r = h * RELAYS // PARTS
            with span(f"waitblocks{r}"):
                if r == 0:
                    drain(xr_s, rs.at[0])
                drain(xr_m.at[r], rm.at[r])
                drain(xr_c.at[r], rc.at[r])
            xf_m[r] = xr_m[r].astype(jnp.float32).reshape(slots * cp, LANES)
            xf_c[r] = xr_c[r].astype(jnp.float32).reshape(slots * 2 * cp, LANES)
        scales = xr_s[:, 0, :]
        s1 = scales[:, 0:1]
        s2 = scales[:, LANES // 4:LANES // 4 + 1]
        s0 = scales[:, LANES // 2:LANES // 2 + 1]
        keep, q1, r1, t1, u1, q2, r2, t2, u2, mine = setup(h)
        with span(f"waitsecond{h}"):
            drain(r2, r2nd.at[h])
            drain(u2, u2nd.at[h])
        top1, top2 = tops
        more = [as_col(u2[b, :, :slots]) for b in range(r2.shape[0])]
        for i in range(h * cq, (h + 1) * cq):
            at = slice(i * LANES, (i + 1) * LANES)
            r, j = i // cp, i % cp
            near = slice((i - h * cq) * LANES, (i - h * cq + 1) * LANES)
            grad = keep[mine, :, near]
            for b in range(r2.shape[0]):
                grad = grad + r2[b, :, near].astype(jnp.float32) * more[b]
            first = xf_c[r, pl.ds(j, slots, stride=2 * cp), :] * s1
            other = xf_c[r, pl.ds(cp + j, slots, stride=2 * cp), :] * s2
            old = xf_m[r, pl.ds(j, slots, stride=cp), :] * s0
            one = 0.9 * first + 0.1 * grad
            two = 0.95 * other + 0.05 * grad * grad
            update = (one * inv_one) / (jnp.sqrt(two * inv_two) + 1e-08) + 0.1 * old
            new = old - 0.01 * update
            nm_out[0, :, at] = new
            wg[0, my_dp, :, at] = new.astype(jnp.bfloat16)
            m1_v[:, at] = one
            m2_v[:, at] = two
            top1 = jnp.maximum(top1, jnp.abs(one))
            top2 = jnp.maximum(top2, jnp.abs(two))
        return top1, top2

    def gathered(chip, h):
        return wg.at[0, chip * 2 + my_c, :, cols(h)]

    def to_chip(h, chip, y, x):
        item = gathered(chip, h)
        pltpu.make_async_remote_copy(
            src_ref=item, dst_ref=item, send_sem=sent.at[12], recv_sem=ra.at[h, chip],
            device_id=(dp_of(y, x, my_c), my_t), device_id_type=MESH,
        ).start()

    def to_partner(h, chip):
        item = gathered(chip, h)
        pltpu.make_async_remote_copy(
            src_ref=item, dst_ref=item, send_sem=sent.at[12], recv_sem=rf.at[0],
            device_id=(partner, my_t), device_id_type=MESH,
        ).start()

    def arrived(h, chip):
        item = gathered(chip, h)
        pltpu.make_async_copy(item, item, ra.at[h, chip]).wait()

    rows_away = [row_away(away) for away in range(1, ny)]
    beside = my_y * 2 + other_x
    above = [y * 2 + my_x for y in rows_away]
    corners = [y * 2 + other_x for y in rows_away]

    def direct(h):
        return 2 * h >= PARTS

    def spread(h):
        to_chip(h, my_chip, my_y, other_x)
        for y in rows_away:
            to_chip(h, my_chip, y, my_x)
        if direct(h):
            for y in rows_away:
                to_chip(h, my_chip, y, other_x)
        to_partner(h, my_chip)

    def landed(h, chip):
        with span(f"arrive{h}"):
            arrived(h, chip)
        to_partner(h, chip)

    def relay(h):
        if direct(h):
            for chip in [beside] + above:
                landed(h, chip)
        elif h % 2 == 0:
            for chip in above:
                with span(f"relay{h}"):
                    arrived(h, chip)
                to_chip(h, chip, my_y, other_x)
                to_partner(h, chip)
            landed(h, beside)
        else:
            with span(f"relay{h}"):
                arrived(h, beside)
            for y in rows_away:
                to_chip(h, beside, y, my_x)
            to_partner(h, beside)
            for chip in above:
                landed(h, chip)

    def finish(h):
        for chip in corners:
            landed(h, chip)

    zero = jnp.zeros((slots, LANES), jnp.float32)
    tops = (zero, zero)
    for h in range(PARTS):
        with span(f"adam{h}"):
            tops = adam(h, tops)
        with span(f"spread{h}"):
            spread(h)
    with span("codes"):
        top1 = jnp.max(tops[0], axis=1, keepdims=True) + 1e-06
        top2 = jnp.max(tops[1], axis=1, keepdims=True) + 1e-06
        ns1_out[...] = as_row(top1)
        ns2_out[...] = as_row(top2)
        inv1 = 1.0 / top1
        inv2 = 1.0 / top2
        for j in range(chunks):
            at = slice(j * LANES, (j + 1) * LANES)
            nc1_out[0, :, at] = (m1_v[:, at] * inv1).astype(jnp.bfloat16)
            nc2_out[0, :, at] = (m2_v[:, at] * inv2).astype(jnp.bfloat16)

    for h in range(PARTS):
        relay(h)
    with span("finish"):
        for h in range(PARTS):
            finish(h)
    with span("drainend"):
        drain(wg.at[0, pl.ds(0, chips)], rf.at[0])
        rest = pl.ds(0, slots - per)
        items = (got, q1_x, q1_y, t1_x, t1_y, q2_x, q2_y, t2_x, t2_y,
                 xs_m.at[:, rest], xs_c.at[:, rest], xs_s.at[rest], wg.at[0, pl.ds(0, 2 * chips - 1)])
        for i, item in enumerate(items):
            drain(item, sent.at[i])


def _write_out(*refs):
    sem = refs[-1]
    count = (len(refs) - 1) // 2
    copies = [pltpu.make_async_copy(refs[i], refs[count + i], sem.at[i]) for i in range(count)]
    for item in copies:
        item.start()
    for item in copies:
        item.wait()


def _bytes(shape, dtype):
    return math.prod(shape) * jnp.dtype(dtype).itemsize


def on_device(send_order, master, first_code, first_scale, second_code, second_scale, grads):
    arrays = (send_order, master, first_code, first_scale, second_code, second_scale, grads)
    nd = lax.axis_size("dp")
    nt = lax.axis_size("tensor")
    slots = master.shape[1]
    width = master.shape[2]
    f32, b16, i16 = jnp.float32, jnp.bfloat16, jnp.int16
    dma = pltpu.SemaphoreType.DMA
    ny = nd // 4
    pairs = PARTS // 2
    wp = width // PARTS
    cp = width // LANES // RELAYS
    arrays = arrays[:6] + (grads.reshape(ny, 2, 2, slots, width),)
    results = (
        ((1, slots, width), f32),
        ((1, slots, width), b16),
        ((1, slots), f32),
        ((1, slots, width), b16),
        ((1, slots), f32),
        ((1, nd, slots, width), b16),
    )
    first_x, first_y = (pairs, 1, ny), (pairs, ny - 1, 2)
    then_x, then_y = (pairs, ny - 1), (pairs, 1)
    data = [(lead + (slots, wp), i16) for lead in (first_x, first_y, first_x, first_y, then_x, then_y, then_x, then_y)]
    sizes = [(lead + (1, LANES), f32) for lead in (first_x, first_y, first_x, first_y, then_x, then_y, then_x, then_y)]
    scratch = [
        ((1, slots), jnp.int32),
        ((1, slots), f32),
        ((1, slots), f32),
        ((slots, width), f32),
        ((slots, width), b16),
        ((slots, width), b16),
        ((RELAYS, slots * cp, LANES), f32),
        ((RELAYS, slots * 2 * cp, LANES), f32),
        ((RELAYS, slots, cp, LANES), i16),
        ((RELAYS, slots, 2 * cp, LANES), b16),
        ((slots, 1, LANES), f32),
        ((RELAYS, slots, cp, LANES), i16),
        ((RELAYS, slots, 2 * cp, LANES), b16),
        ((slots, 1, LANES), f32),
        ((ny, 2, slots, width), b16),
        ((PARTS, ny, 2, slots, wp), b16),
        ((pairs, ny, slots, wp), f32),
        ((pairs, 2, slots, wp), f32),
        *data,
        *sizes,
        ((slots, width), f32),
        ((slots, width), f32),
    ]
    grant = sum(_bytes(*item) for item in scratch) + sum(_bytes(*item) for item in results) + slots * 8192 + 6 * 1024 * 1024
    held = pl.pallas_call(
        functools.partial(_kernel, nd, nt, slots, width),
        out_shape=tuple(pltpu.VMEM(*item) for item in results),
        in_specs=[pl.BlockSpec(memory_space=pltpu.HBM)] * 7,
        out_specs=[pl.BlockSpec(memory_space=pltpu.VMEM)] * 6,
        scratch_shapes=[
            *(pltpu.VMEM(*item) for item in scratch),
            dma((6,)), dma((1,)), dma((13,)), dma((RELAYS,)), dma((RELAYS,)), dma((1,)), dma((PARTS,)),
            dma((PARTS,)), dma((PARTS,)), dma((PARTS,)), dma((PARTS,)), dma((PARTS, 2 * ny)), dma((1,)),
            pltpu.SemaphoreType.REGULAR((nt,)),
        ],
        compiler_params=pltpu.CompilerParams(collective_id=0, has_side_effects=True, vmem_limit_bytes=grant),
        name="relayout_adam",
    )(*(pltpu.with_memory_space_constraint(item, pltpu.HBM) for item in arrays))
    return pl.pallas_call(
        _write_out,
        out_shape=tuple(jax.ShapeDtypeStruct(*item) for item in results),
        in_specs=[pl.BlockSpec(memory_space=pltpu.VMEM)] * len(results),
        out_specs=[pl.BlockSpec(memory_space=pltpu.HBM)] * len(results),
        scratch_shapes=[dma((len(results),))],
        compiler_params=pltpu.CompilerParams(vmem_limit_bytes=2 * 1024 * 1024),
        name="write_out",
    )(*(pltpu.with_memory_space_constraint(item, pltpu.VMEM) for item in held))


def solution(mesh):
    placed = (
        P(("dp", "tensor"), None),
        P(("dp", "tensor"), None, None),
        P(("dp", "tensor"), None, None),
        P(("dp", "tensor"), None),
        P(("dp", "tensor"), None, None),
        P(("dp", "tensor"), None),
        P("dp", "tensor", None, None, None),
    )
    return jax.shard_map(
        on_device,
        mesh=mesh,
        in_specs=placed,
        out_specs=(
            P(("dp", "tensor"), None, None),
            P(("dp", "tensor"), None, None),
            P(("dp", "tensor"), None),
            P(("dp", "tensor"), None, None),
            P(("dp", "tensor"), None),
            P("tensor", None, None, None),
        ),
        check_vma=False,
    )
```

```python
from contextlib import nullcontext as span
import functools
import math

import jax
import jax.numpy as jnp
from jax import lax
from jax.experimental import pallas as pl
from jax.experimental.pallas import tpu as pltpu
from jax.sharding import PartitionSpec as P

STEP = 10
LANES = 128
RELAYS = 2
PARTS = 4
LEVELS = 32767.0
TINY = 1e-30
MESH = pl.DeviceIdType.MESH


def _kernel(nd, nt, slots, width, order_hbm, m_hbm, c1_hbm, s1_hbm, c2_hbm, s2_hbm, g_hbm,
            nm_out, nc1_out, ns1_out, nc2_out, ns2_out, wg,
            order_v, s1_v, s2_v, m_v, c1_v, c2_v, xf_m, xf_c,
            xs_m, xs_c, xs_s, xr_m, xr_c, xr_s, own, got,
            keep_x, keep_y, q1_x, q1_y, r1_x, r1_y, q2_x, q2_y, r2_x, r2_y,
            t1_x, t1_y, u1_x, u1_y, t2_x, t2_y, u2_x, u2_y, m1_v, m2_v,
            in_sem, own_sem, sent, rm, rc, rs, rp, r1st, u1st, r2nd, u2nd, ra, rf, plane_in):
    n = nd * nt
    per = slots // n
    chunks = width // LANES
    cp = chunks // RELAYS
    cq = chunks // PARTS
    wr = width // RELAYS
    wp = width // PARTS
    ny = nd // 4
    chips = 2 * ny
    my_dp = lax.axis_index("dp")
    my_t = lax.axis_index("tensor")
    me = my_dp * nt + my_t
    my_c = lax.rem(my_dp, 2)
    my_chip = my_dp // 2
    my_x = lax.rem(my_chip, 2)
    my_y = my_chip // 2
    other_c = 1 - my_c
    other_x = 1 - my_x
    partner = my_dp + 1 - 2 * my_c

    def dp_of(y, x, c):
        return (y * 2 + x) * 2 + c

    def row_away(away):
        return lax.rem(my_y + away, ny)

    barrier = pltpu.get_barrier_semaphore()

    def tell(sem, up):
        where = (my_dp, my_t + 1 if up else my_t - 1)

        @pl.when(my_t < nt - 1 if up else my_t > 0)
        def _():
            pl.semaphore_signal(sem, inc=1, device_id=where, device_id_type=MESH)

    def greet(k, carry):
        pl.semaphore_signal(barrier, inc=1, device_id=(lax.rem(my_dp + k, nd), my_t), device_id_type=MESH)
        return carry

    tell(barrier, True)
    tell(barrier, False)
    lax.fori_loop(1, nd, greet, 0)

    loads = [
        pltpu.make_async_copy(order_hbm, order_v, in_sem.at[0]),
        pltpu.make_async_copy(m_hbm.at[0], m_v, in_sem.at[3]),
        pltpu.make_async_copy(s1_hbm, s1_v, in_sem.at[1]),
        pltpu.make_async_copy(s2_hbm, s2_v, in_sem.at[2]),
        pltpu.make_async_copy(c1_hbm.at[0], c1_v, in_sem.at[4]),
        pltpu.make_async_copy(c2_hbm.at[0], c2_v, in_sem.at[5]),
    ]
    for item in loads:
        item.start()

    def cols(h):
        return pl.ds(h * wp, wp)

    def wide(r):
        return pl.ds(r * wr, wr)

    def drain(ref, sem):
        pltpu.make_async_copy(ref, ref, sem).wait()

    load_own = pltpu.make_async_copy(g_hbm.at[:, :, my_c], own, own_sem.at[0])

    def send_pairs(h):
        pltpu.make_async_remote_copy(
            src_ref=g_hbm.at[:, :, other_c, :, cols(h)], dst_ref=got.at[h],
            send_sem=sent.at[0], recv_sem=rp.at[h], device_id=(partner, my_t), device_id_type=MESH,
        ).start()

    with span("barrier"):
        beside_me = jnp.where(my_t > 0, 1, 0) + jnp.where(my_t < nt - 1, 1, 0)
        pl.semaphore_wait(barrier, nd - 1 + beside_me)

    tell(plane_in.at[my_t], True)
    tell(plane_in.at[my_t], False)
    for h in range(PARTS):
        send_pairs(h)
    load_own.start()

    with span("loads"):
        for item in loads:
            item.wait()

    eye = lax.broadcasted_iota(jnp.int32, (slots, slots), 0) == lax.broadcasted_iota(jnp.int32, (slots, slots), 1)

    def as_row(col):
        return jnp.sum(jnp.where(eye, col, 0.0), axis=0, keepdims=True)

    def as_col(row):
        return jnp.sum(jnp.where(eye, row, 0.0), axis=1, keepdims=True)

    def scale_of(x):
        return (jnp.max(jnp.abs(x), axis=1, keepdims=True) + TINY) * (1.0 / LEVELS)

    with span("prep"):
        lane = lax.broadcasted_iota(jnp.int32, (slots, slots), 1)
        order_col = as_col(order_v[...].astype(jnp.float32))
        pick = order_col == lane.astype(jnp.float32)

        def picked(row):
            return jnp.sum(jnp.where(pick, row, 0.0), axis=1, keepdims=True)

        m_scale = scale_of(m_v[...])
        m_inv = 1.0 / m_scale
        place = lax.broadcasted_iota(jnp.int32, (slots, LANES), 1)
        both = jnp.where(place < LANES // 4, picked(s1_v[...]), picked(s2_v[...]))
        xs_s[:, 0, :] = jnp.where(place < LANES // 2, both, picked(as_row(m_scale)))
        select = jnp.where(pick, 1.0, 0.0).astype(jnp.bfloat16)

    def take(x):
        return jnp.dot(select, x, preferred_element_type=jnp.float32)

    def stage(r):
        level = jnp.round(m_v[:, wide(r)] * m_inv)
        high = jnp.round(level * (1.0 / 256.0))
        low = level - 256.0 * high
        xm = 256.0 * take(high.astype(jnp.bfloat16)) + take(low.astype(jnp.bfloat16))
        x1 = take(c1_v[:, wide(r)])
        x2 = take(c2_v[:, wide(r)])
        for j in range(cp):
            piece = slice(j * LANES, (j + 1) * LANES)
            xf_m[r, pl.ds(j, slots, stride=cp), :] = xm[:, piece]
            xf_c[r, pl.ds(j, slots, stride=2 * cp), :] = x1[:, piece]
            xf_c[r, pl.ds(cp + j, slots, stride=2 * cp), :] = x2[:, piece]
        xs_m[r] = xf_m[r].reshape(slots, cp, LANES).astype(jnp.int16)
        xs_c[r] = xf_c[r].reshape(slots, 2 * cp, LANES).astype(jnp.bfloat16)

    with span("stage"):
        for r in range(RELAYS):
            stage(r)

    def send_block(r, t, dp):
        dst = dp * nt + t
        theirs, mine = pl.ds(dst * per, per), pl.ds(me * per, per)
        where = (dp, t)
        pltpu.make_async_remote_copy(
            src_ref=xs_m.at[r, theirs], dst_ref=xr_m.at[r, mine],
            send_sem=sent.at[9], recv_sem=rm.at[r], device_id=where, device_id_type=MESH,
        ).start()
        pltpu.make_async_remote_copy(
            src_ref=xs_c.at[r, theirs], dst_ref=xr_c.at[r, mine],
            send_sem=sent.at[10], recv_sem=rc.at[r], device_id=where, device_id_type=MESH,
        ).start()
        if r == 0:
            pltpu.make_async_remote_copy(
                src_ref=xs_s.at[theirs], dst_ref=xr_s.at[mine],
                send_sem=sent.at[11], recv_sem=rs.at[0], device_id=where, device_id_type=MESH,
            ).start()

    early = 2 * my_t < nt

    def hear(t):
        @pl.when(my_t != t)
        def _():
            pl.semaphore_wait(plane_in.at[t], 1)

        pl.when(t < my_t)(functools.partial(tell, plane_in.at[t], True))
        pl.when(t > my_t)(functools.partial(tell, plane_in.at[t], False))

    def send_blocks(i):
        t = jnp.where(early, i, lax.rem(nt - i, nt))
        if i > 0:
            hear(t)
        for r in range(RELAYS):
            def one(k, carry, r=r):
                send_block(r, t, lax.rem(my_dp + k, nd))
                return carry

            lax.fori_loop(jnp.where(my_t == t, 1, 0), nd, one, 0)

    def keep_blocks():
        mine = pl.ds(me * per, per)
        pltpu.make_async_copy(xs_s.at[mine], xr_s.at[mine], rs.at[0]).start()
        for r in range(RELAYS):
            pltpu.make_async_copy(xs_m.at[r, mine], xr_m.at[r, mine], rm.at[r]).start()
            pltpu.make_async_copy(xs_c.at[r, mine], xr_c.at[r, mine], rc.at[r]).start()

    def setup(h):
        k = h // 2
        if h % 2 == 0:
            return (keep_x.at[k], q1_x.at[k], r1_x.at[k], t1_x.at[k], u1_x.at[k],
                    q2_x.at[k], r2_x.at[k], t2_x.at[k], u2_x.at[k], my_y)
        return (keep_y.at[k], q1_y.at[k], r1_y.at[k], t1_y.at[k], u1_y.at[k],
                q2_y.at[k], r2_y.at[k], t2_y.at[k], u2_y.at[k], my_x)

    def at_first(h, a):
        return (my_y, other_x) if h % 2 == 0 else (row_away(a + 1), my_x)

    def at_second(h, b):
        return (row_away(b + 1), my_x) if h % 2 == 0 else (my_y, other_x)

    def slab(h, first, t):
        y, x = first
        return (t, x) if h % 2 == 0 else (y, t)

    def pair_sum(h, y, x):
        return own[y, x, :, cols(h)].astype(jnp.float32) + got[h, y, x].astype(jnp.float32)

    def pack(v, q, t):
        scale = scale_of(v)
        q[...] = jnp.round(v * (1.0 / scale)).astype(jnp.int16)
        t[:, :slots] = as_row(scale)

    def unpack(r, u):
        return r[...].astype(jnp.float32) * as_col(u[:, :slots])

    def remote(src, dst, send, recv, place):
        y, x = place
        pltpu.make_async_remote_copy(
            src_ref=src, dst_ref=dst, send_sem=sent.at[send], recv_sem=recv,
            device_id=(dp_of(y, x, my_c), my_t), device_id_type=MESH,
        ).start()

    def first_stop(h):
        keep, q1, r1, t1, u1 = setup(h)[:5]
        with span(f"waitpair{h}"):
            drain(got.at[h], rp.at[h])
        for a in range(q1.shape[0]):
            place = at_first(h, a)
            for t in range(q1.shape[1]):
                pack(pair_sum(h, *slab(h, place, t)), q1.at[a, t], t1.at[a, t])
            remote(q1.at[a], r1.at[a], 1 + h % 2, r1st.at[h], place)
            remote(t1.at[a], u1.at[a], 3 + h % 2, u1st.at[h], place)
        for t in range(q1.shape[1]):
            keep[t] = pair_sum(h, *slab(h, (my_y, my_x), t))

    def second_stop(h):
        keep, q1, r1, t1, u1, q2, r2, t2, u2, mine = setup(h)
        with span(f"waitfirst{h}"):
            drain(r1, r1st.at[h])
            drain(u1, u1st.at[h])

        def total(t):
            return functools.reduce(jnp.add, [unpack(r1.at[a, t], u1.at[a, t]) for a in range(r1.shape[0])], keep[t])

        for b in range(q2.shape[0]):
            y, x = at_second(h, b)
            pack(total(y if h % 2 == 0 else x), q2.at[b], t2.at[b])
            remote(q2.at[b], r2.at[b], 5 + h % 2, r2nd.at[h], (y, x))
            remote(t2.at[b], u2.at[b], 7 + h % 2, u2nd.at[h], (y, x))
        keep[mine] = total(mine)

    with span("hear0"):
        hear(0)
    load_own.wait()
    for h in range(PARTS):
        with span(f"first{h}"):
            first_stop(h)

    def second_stops():
        for h in range(PARTS // 2):
            with span(f"second{h}"):
                second_stop(h)

    with span("sendblocks"):
        for i in range(nt - 1):
            send_blocks(i)
        keep_blocks()
    pl.when(early)(second_stops)
    with span("sendlast"):
        send_blocks(nt - 1)
    pl.when(jnp.logical_not(early))(second_stops)
    for h in range(PARTS // 2, PARTS):
        with span(f"second{h}"):
            second_stop(h)

    inv_one = 1.0 / (1.0 - 0.9**STEP)
    inv_two = 1.0 / (1.0 - 0.95**STEP)

    def adam(h, tops):
        if h * RELAYS % PARTS == 0:
            r = h * RELAYS // PARTS
            with span(f"waitblocks{r}"):
                if r == 0:
                    drain(xr_s, rs.at[0])
                drain(xr_m.at[r], rm.at[r])
                drain(xr_c.at[r], rc.at[r])
            xf_m[r] = xr_m[r].astype(jnp.float32).reshape(slots * cp, LANES)
            xf_c[r] = xr_c[r].astype(jnp.float32).reshape(slots * 2 * cp, LANES)
        scales = xr_s[:, 0, :]
        s1 = scales[:, 0:1]
        s2 = scales[:, LANES // 4:LANES // 4 + 1]
        s0 = scales[:, LANES // 2:LANES // 2 + 1]
        keep, q1, r1, t1, u1, q2, r2, t2, u2, mine = setup(h)
        with span(f"waitsecond{h}"):
            drain(r2, r2nd.at[h])
            drain(u2, u2nd.at[h])
        top1, top2 = tops
        more = [as_col(u2[b, :, :slots]) for b in range(r2.shape[0])]
        for i in range(h * cq, (h + 1) * cq):
            at = slice(i * LANES, (i + 1) * LANES)
            r, j = i // cp, i % cp
            near = slice((i - h * cq) * LANES, (i - h * cq + 1) * LANES)
            grad = keep[mine, :, near]
            for b in range(r2.shape[0]):
                grad = grad + r2[b, :, near].astype(jnp.float32) * more[b]
            first = xf_c[r, pl.ds(j, slots, stride=2 * cp), :] * s1
            other = xf_c[r, pl.ds(cp + j, slots, stride=2 * cp), :] * s2
            old = xf_m[r, pl.ds(j, slots, stride=cp), :] * s0
            one = 0.9 * first + 0.1 * grad
            two = 0.95 * other + 0.05 * grad * grad
            update = (one * inv_one) / (jnp.sqrt(two * inv_two) + 1e-08) + 0.1 * old
            new = old - 0.01 * update
            nm_out[0, :, at] = new
            wg[0, my_dp, :, at] = new.astype(jnp.bfloat16)
            m1_v[:, at] = one
            m2_v[:, at] = two
            top1 = jnp.maximum(top1, jnp.abs(one))
            top2 = jnp.maximum(top2, jnp.abs(two))
        return top1, top2

    def gathered(chip, h):
        return wg.at[0, chip * 2 + my_c, :, cols(h)]

    def to_chip(h, chip, y, x):
        item = gathered(chip, h)
        pltpu.make_async_remote_copy(
            src_ref=item, dst_ref=item, send_sem=sent.at[12], recv_sem=ra.at[h, chip],
            device_id=(dp_of(y, x, my_c), my_t), device_id_type=MESH,
        ).start()

    def to_partner(h, chip):
        item = gathered(chip, h)
        pltpu.make_async_remote_copy(
            src_ref=item, dst_ref=item, send_sem=sent.at[12], recv_sem=rf.at[0],
            device_id=(partner, my_t), device_id_type=MESH,
        ).start()

    def arrived(h, chip):
        item = gathered(chip, h)
        pltpu.make_async_copy(item, item, ra.at[h, chip]).wait()

    rows_away = [row_away(away) for away in range(1, ny)]
    beside = my_y * 2 + other_x
    above = [y * 2 + my_x for y in rows_away]
    corners = [y * 2 + other_x for y in rows_away]

    def direct(h):
        return 2 * h >= PARTS

    def spread(h):
        to_chip(h, my_chip, my_y, other_x)
        for y in rows_away:
            to_chip(h, my_chip, y, my_x)
        if direct(h):
            for y in rows_away:
                to_chip(h, my_chip, y, other_x)
        to_partner(h, my_chip)

    def landed(h, chip):
        with span(f"arrive{h}"):
            arrived(h, chip)
        to_partner(h, chip)

    def relay(h):
        if direct(h):
            for chip in [beside] + above:
                landed(h, chip)
        elif h % 2 == 0:
            for chip in above:
                with span(f"relay{h}"):
                    arrived(h, chip)
                to_chip(h, chip, my_y, other_x)
                to_partner(h, chip)
            landed(h, beside)
        else:
            with span(f"relay{h}"):
                arrived(h, beside)
            for y in rows_away:
                to_chip(h, beside, y, my_x)
            to_partner(h, beside)
            for chip in above:
                landed(h, chip)

    def finish(h):
        for chip in corners:
            landed(h, chip)

    zero = jnp.zeros((slots, LANES), jnp.float32)
    tops = (zero, zero)
    for h in range(PARTS):
        with span(f"adam{h}"):
            tops = adam(h, tops)
        with span(f"spread{h}"):
            spread(h)
    with span("codes"):
        top1 = jnp.max(tops[0], axis=1, keepdims=True) + 1e-06
        top2 = jnp.max(tops[1], axis=1, keepdims=True) + 1e-06
        ns1_out[...] = as_row(top1)
        ns2_out[...] = as_row(top2)
        inv1 = 1.0 / top1
        inv2 = 1.0 / top2
        for j in range(chunks):
            at = slice(j * LANES, (j + 1) * LANES)
            nc1_out[0, :, at] = (m1_v[:, at] * inv1).astype(jnp.bfloat16)
            nc2_out[0, :, at] = (m2_v[:, at] * inv2).astype(jnp.bfloat16)

    for h in range(PARTS):
        relay(h)
    with span("finish"):
        for h in range(PARTS):
            finish(h)
    with span("drainend"):
        drain(wg.at[0, pl.ds(0, chips)], rf.at[0])
        rest = pl.ds(0, slots - per)
        items = (got, q1_x, q1_y, t1_x, t1_y, q2_x, q2_y, t2_x, t2_y,
                 xs_m.at[:, rest], xs_c.at[:, rest], xs_s.at[rest], wg.at[0, pl.ds(0, 2 * chips - 1)])
        for i, item in enumerate(items):
            drain(item, sent.at[i])


def _write_out(*refs):
    sem = refs[-1]
    count = (len(refs) - 1) // 2
    copies = [pltpu.make_async_copy(refs[i], refs[count + i], sem.at[i]) for i in range(count)]
    for item in copies:
        item.start()
    for item in copies:
        item.wait()


def _bytes(shape, dtype):
    return math.prod(shape) * jnp.dtype(dtype).itemsize


def on_device(send_order, master, first_code, first_scale, second_code, second_scale, grads):
    arrays = (send_order, master, first_code, first_scale, second_code, second_scale, grads)
    nd = lax.axis_size("dp")
    nt = lax.axis_size("tensor")
    slots = master.shape[1]
    width = master.shape[2]
    f32, b16, i16 = jnp.float32, jnp.bfloat16, jnp.int16
    dma = pltpu.SemaphoreType.DMA
    ny = nd // 4
    pairs = PARTS // 2
    wp = width // PARTS
    cp = width // LANES // RELAYS
    arrays = arrays[:6] + (grads.reshape(ny, 2, 2, slots, width),)
    results = (
        ((1, slots, width), f32),
        ((1, slots, width), b16),
        ((1, slots), f32),
        ((1, slots, width), b16),
        ((1, slots), f32),
        ((1, nd, slots, width), b16),
    )
    first_x, first_y = (pairs, 1, ny), (pairs, ny - 1, 2)
    then_x, then_y = (pairs, ny - 1), (pairs, 1)
    data = [(lead + (slots, wp), i16) for lead in (first_x, first_y, first_x, first_y, then_x, then_y, then_x, then_y)]
    sizes = [(lead + (1, LANES), f32) for lead in (first_x, first_y, first_x, first_y, then_x, then_y, then_x, then_y)]
    scratch = [
        ((1, slots), jnp.int32),
        ((1, slots), f32),
        ((1, slots), f32),
        ((slots, width), f32),
        ((slots, width), b16),
        ((slots, width), b16),
        ((RELAYS, slots * cp, LANES), f32),
        ((RELAYS, slots * 2 * cp, LANES), f32),
        ((RELAYS, slots, cp, LANES), i16),
        ((RELAYS, slots, 2 * cp, LANES), b16),
        ((slots, 1, LANES), f32),
        ((RELAYS, slots, cp, LANES), i16),
        ((RELAYS, slots, 2 * cp, LANES), b16),
        ((slots, 1, LANES), f32),
        ((ny, 2, slots, width), b16),
        ((PARTS, ny, 2, slots, wp), b16),
        ((pairs, ny, slots, wp), f32),
        ((pairs, 2, slots, wp), f32),
        *data,
        *sizes,
        ((slots, width), f32),
        ((slots, width), f32),
    ]
    grant = sum(_bytes(*item) for item in scratch) + sum(_bytes(*item) for item in results) + slots * 8192 + 6 * 1024 * 1024
    held = pl.pallas_call(
        functools.partial(_kernel, nd, nt, slots, width),
        out_shape=tuple(pltpu.VMEM(*item) for item in results),
        in_specs=[pl.BlockSpec(memory_space=pltpu.HBM)] * 7,
        out_specs=[pl.BlockSpec(memory_space=pltpu.VMEM)] * 6,
        scratch_shapes=[
            *(pltpu.VMEM(*item) for item in scratch),
            dma((6,)), dma((1,)), dma((13,)), dma((RELAYS,)), dma((RELAYS,)), dma((1,)), dma((PARTS,)),
            dma((PARTS,)), dma((PARTS,)), dma((PARTS,)), dma((PARTS,)), dma((PARTS, 2 * ny)), dma((1,)),
            pltpu.SemaphoreType.REGULAR((nt,)),
        ],
        compiler_params=pltpu.CompilerParams(collective_id=0, has_side_effects=True, vmem_limit_bytes=grant),
        name="relayout_adam",
    )(*(pltpu.with_memory_space_constraint(item, pltpu.HBM) for item in arrays))
    return pl.pallas_call(
        _write_out,
        out_shape=tuple(jax.ShapeDtypeStruct(*item) for item in results),
        in_specs=[pl.BlockSpec(memory_space=pltpu.VMEM)] * len(results),
        out_specs=[pl.BlockSpec(memory_space=pltpu.HBM)] * len(results),
        scratch_shapes=[dma((len(results),))],
        compiler_params=pltpu.CompilerParams(vmem_limit_bytes=2 * 1024 * 1024),
        name="write_out",
    )(*(pltpu.with_memory_space_constraint(item, pltpu.VMEM) for item in held))


def solution(mesh):
    placed = (
        P(("dp", "tensor"), None),
        P(("dp", "tensor"), None, None),
        P(("dp", "tensor"), None, None),
        P(("dp", "tensor"), None),
        P(("dp", "tensor"), None, None),
        P(("dp", "tensor"), None),
        P("dp", "tensor", None, None, None),
    )
    return jax.shard_map(
        on_device,
        mesh=mesh,
        in_specs=placed,
        out_specs=(
            P(("dp", "tensor"), None, None),
            P(("dp", "tensor"), None, None),
            P(("dp", "tensor"), None),
            P(("dp", "tensor"), None, None),
            P(("dp", "tensor"), None),
            P("tensor", None, None, None),
        ),
        check_vma=False,
    )
```

```python
from contextlib import nullcontext as span
import functools
import math

import jax
import jax.numpy as jnp
from jax import lax
from jax.experimental import pallas as pl
from jax.experimental.pallas import tpu as pltpu
from jax.sharding import PartitionSpec as P

STEP = 10
LANES = 128
RELAYS = 2
PARTS = 4
LEVELS = 32767.0
TINY = 1e-30
MESH = pl.DeviceIdType.MESH


def _kernel(nd, nt, slots, width, order_hbm, m_hbm, c1_hbm, s1_hbm, c2_hbm, s2_hbm, g_hbm,
            nm_out, nc1_out, ns1_out, nc2_out, ns2_out, wg,
            order_v, s1_v, s2_v, m_v, c1_v, c2_v, xf_m, xf_c,
            xs_m, xs_c, xs_s, xr_m, xr_c, xr_s, own, got,
            keep_x, keep_y, q1_x, q1_y, r1_x, r1_y, q2_x, q2_y, r2_x, r2_y,
            t1_x, t1_y, u1_x, u1_y, t2_x, t2_y, u2_x, u2_y, m1_v, m2_v,
            in_sem, own_sem, sent, rm, rc, rs, rp, r1st, u1st, r2nd, u2nd, ra, rf, plane_in):
    n = nd * nt
    per = slots // n
    chunks = width // LANES
    cp = chunks // RELAYS
    cq = chunks // PARTS
    wr = width // RELAYS
    wp = width // PARTS
    ny = nd // 4
    chips = 2 * ny
    my_dp = lax.axis_index("dp")
    my_t = lax.axis_index("tensor")
    me = my_dp * nt + my_t
    my_c = lax.rem(my_dp, 2)
    my_chip = my_dp // 2
    my_x = lax.rem(my_chip, 2)
    my_y = my_chip // 2
    other_c = 1 - my_c
    other_x = 1 - my_x
    partner = my_dp + 1 - 2 * my_c

    def dp_of(y, x, c):
        return (y * 2 + x) * 2 + c

    def row_away(away):
        return lax.rem(my_y + away, ny)

    barrier = pltpu.get_barrier_semaphore()

    def tell(sem, up):
        where = (my_dp, my_t + 1 if up else my_t - 1)

        @pl.when(my_t < nt - 1 if up else my_t > 0)
        def _():
            pl.semaphore_signal(sem, inc=1, device_id=where, device_id_type=MESH)

    def greet(k, carry):
        pl.semaphore_signal(barrier, inc=1, device_id=(lax.rem(my_dp + k, nd), my_t), device_id_type=MESH)
        return carry

    tell(barrier, True)
    tell(barrier, False)
    lax.fori_loop(1, nd, greet, 0)

    loads = [
        pltpu.make_async_copy(order_hbm, order_v, in_sem.at[0]),
        pltpu.make_async_copy(m_hbm.at[0], m_v, in_sem.at[3]),
        pltpu.make_async_copy(s1_hbm, s1_v, in_sem.at[1]),
        pltpu.make_async_copy(s2_hbm, s2_v, in_sem.at[2]),
        pltpu.make_async_copy(c1_hbm.at[0], c1_v, in_sem.at[4]),
        pltpu.make_async_copy(c2_hbm.at[0], c2_v, in_sem.at[5]),
    ]
    for item in loads:
        item.start()

    def cols(h):
        return pl.ds(h * wp, wp)

    def wide(r):
        return pl.ds(r * wr, wr)

    def drain(ref, sem):
        pltpu.make_async_copy(ref, ref, sem).wait()

    load_own = pltpu.make_async_copy(g_hbm.at[:, :, my_c], own, own_sem.at[0])

    def send_pairs(h):
        pltpu.make_async_remote_copy(
            src_ref=g_hbm.at[:, :, other_c, :, cols(h)], dst_ref=got.at[h],
            send_sem=sent.at[0], recv_sem=rp.at[h], device_id=(partner, my_t), device_id_type=MESH,
        ).start()

    with span("barrier"):
        beside_me = jnp.where(my_t > 0, 1, 0) + jnp.where(my_t < nt - 1, 1, 0)
        pl.semaphore_wait(barrier, nd - 1 + beside_me)

    tell(plane_in.at[my_t], True)
    tell(plane_in.at[my_t], False)
    for h in range(PARTS):
        send_pairs(h)
    load_own.start()

    with span("loads"):
        for item in loads:
            item.wait()

    eye = lax.broadcasted_iota(jnp.int32, (slots, slots), 0) == lax.broadcasted_iota(jnp.int32, (slots, slots), 1)

    def as_row(col):
        return jnp.sum(jnp.where(eye, col, 0.0), axis=0, keepdims=True)

    def as_col(row):
        return jnp.sum(jnp.where(eye, row, 0.0), axis=1, keepdims=True)

    def scale_of(x):
        return (jnp.max(jnp.abs(x), axis=1, keepdims=True) + TINY) * (1.0 / LEVELS)

    with span("prep"):
        lane = lax.broadcasted_iota(jnp.int32, (slots, slots), 1)
        order_col = as_col(order_v[...].astype(jnp.float32))
        pick = order_col == lane.astype(jnp.float32)

        def picked(row):
            return jnp.sum(jnp.where(pick, row, 0.0), axis=1, keepdims=True)

        m_scale = scale_of(m_v[...])
        m_inv = 1.0 / m_scale
        place = lax.broadcasted_iota(jnp.int32, (slots, LANES), 1)
        both = jnp.where(place < LANES // 4, picked(s1_v[...]), picked(s2_v[...]))
        xs_s[:, 0, :] = jnp.where(place < LANES // 2, both, picked(as_row(m_scale)))
        select = jnp.where(pick, 1.0, 0.0).astype(jnp.bfloat16)

    def take(x):
        return jnp.dot(select, x, preferred_element_type=jnp.float32)

    def stage(r):
        level = jnp.round(m_v[:, wide(r)] * m_inv)
        high = jnp.round(level * (1.0 / 256.0))
        low = level - 256.0 * high
        xm = 256.0 * take(high.astype(jnp.bfloat16)) + take(low.astype(jnp.bfloat16))
        x1 = take(c1_v[:, wide(r)])
        x2 = take(c2_v[:, wide(r)])
        for j in range(cp):
            piece = slice(j * LANES, (j + 1) * LANES)
            xf_m[r, pl.ds(j, slots, stride=cp), :] = xm[:, piece]
            xf_c[r, pl.ds(j, slots, stride=2 * cp), :] = x1[:, piece]
            xf_c[r, pl.ds(cp + j, slots, stride=2 * cp), :] = x2[:, piece]
        xs_m[r] = xf_m[r].reshape(slots, cp, LANES).astype(jnp.int16)
        xs_c[r] = xf_c[r].reshape(slots, 2 * cp, LANES).astype(jnp.bfloat16)

    with span("stage"):
        for r in range(RELAYS):
            stage(r)

    def send_block(r, t, dp):
        dst = dp * nt + t
        theirs, mine = pl.ds(dst * per, per), pl.ds(me * per, per)
        where = (dp, t)
        pltpu.make_async_remote_copy(
            src_ref=xs_m.at[r, theirs], dst_ref=xr_m.at[r, mine],
            send_sem=sent.at[9], recv_sem=rm.at[r], device_id=where, device_id_type=MESH,
        ).start()
        pltpu.make_async_remote_copy(
            src_ref=xs_c.at[r, theirs], dst_ref=xr_c.at[r, mine],
            send_sem=sent.at[10], recv_sem=rc.at[r], device_id=where, device_id_type=MESH,
        ).start()
        if r == 0:
            pltpu.make_async_remote_copy(
                src_ref=xs_s.at[theirs], dst_ref=xr_s.at[mine],
                send_sem=sent.at[11], recv_sem=rs.at[0], device_id=where, device_id_type=MESH,
            ).start()

    early = 2 * my_t < nt

    def hear(t):
        @pl.when(my_t != t)
        def _():
            pl.semaphore_wait(plane_in.at[t], 1)

        pl.when(t < my_t)(functools.partial(tell, plane_in.at[t], True))
        pl.when(t > my_t)(functools.partial(tell, plane_in.at[t], False))

    def send_blocks(i):
        t = jnp.where(early, i, lax.rem(nt - i, nt))
        if i > 0:
            hear(t)
        for r in range(RELAYS):
            def one(k, carry, r=r):
                send_block(r, t, lax.rem(my_dp + k, nd))
                return carry

            lax.fori_loop(jnp.where(my_t == t, 1, 0), nd, one, 0)

    def keep_blocks():
        mine = pl.ds(me * per, per)
        pltpu.make_async_copy(xs_s.at[mine], xr_s.at[mine], rs.at[0]).start()
        for r in range(RELAYS):
            pltpu.make_async_copy(xs_m.at[r, mine], xr_m.at[r, mine], rm.at[r]).start()
            pltpu.make_async_copy(xs_c.at[r, mine], xr_c.at[r, mine], rc.at[r]).start()

    def setup(h):
        k = h // 2
        if h % 2 == 0:
            return (keep_x.at[k], q1_x.at[k], r1_x.at[k], t1_x.at[k], u1_x.at[k],
                    q2_x.at[k], r2_x.at[k], t2_x.at[k], u2_x.at[k], my_y)
        return (keep_y.at[k], q1_y.at[k], r1_y.at[k], t1_y.at[k], u1_y.at[k],
                q2_y.at[k], r2_y.at[k], t2_y.at[k], u2_y.at[k], my_x)

    def at_first(h, a):
        return (my_y, other_x) if h % 2 == 0 else (row_away(a + 1), my_x)

    def at_second(h, b):
        return (row_away(b + 1), my_x) if h % 2 == 0 else (my_y, other_x)

    def slab(h, first, t):
        y, x = first
        return (t, x) if h % 2 == 0 else (y, t)

    def pair_sum(h, y, x):
        return own[y, x, :, cols(h)].astype(jnp.float32) + got[h, y, x].astype(jnp.float32)

    def pack(v, q, t):
        scale = scale_of(v)
        q[...] = jnp.round(v * (1.0 / scale)).astype(jnp.int16)
        t[:, :slots] = as_row(scale)

    def unpack(r, u):
        return r[...].astype(jnp.float32) * as_col(u[:, :slots])

    def remote(src, dst, send, recv, place):
        y, x = place
        pltpu.make_async_remote_copy(
            src_ref=src, dst_ref=dst, send_sem=sent.at[send], recv_sem=recv,
            device_id=(dp_of(y, x, my_c), my_t), device_id_type=MESH,
        ).start()

    def first_stop(h):
        keep, q1, r1, t1, u1 = setup(h)[:5]
        with span(f"waitpair{h}"):
            drain(got.at[h], rp.at[h])
        for a in range(q1.shape[0]):
            place = at_first(h, a)
            for t in range(q1.shape[1]):
                pack(pair_sum(h, *slab(h, place, t)), q1.at[a, t], t1.at[a, t])
            remote(q1.at[a], r1.at[a], 1 + h % 2, r1st.at[h], place)
            remote(t1.at[a], u1.at[a], 3 + h % 2, u1st.at[h], place)
        for t in range(q1.shape[1]):
            keep[t] = pair_sum(h, *slab(h, (my_y, my_x), t))

    def second_stop(h):
        keep, q1, r1, t1, u1, q2, r2, t2, u2, mine = setup(h)
        with span(f"waitfirst{h}"):
            drain(r1, r1st.at[h])
            drain(u1, u1st.at[h])

        def total(t):
            return functools.reduce(jnp.add, [unpack(r1.at[a, t], u1.at[a, t]) for a in range(r1.shape[0])], keep[t])

        for b in range(q2.shape[0]):
            y, x = at_second(h, b)
            pack(total(y if h % 2 == 0 else x), q2.at[b], t2.at[b])
            remote(q2.at[b], r2.at[b], 5 + h % 2, r2nd.at[h], (y, x))
            remote(t2.at[b], u2.at[b], 7 + h % 2, u2nd.at[h], (y, x))
        keep[mine] = total(mine)

    with span("hear0"):
        hear(0)
    load_own.wait()
    for h in range(PARTS):
        with span(f"first{h}"):
            first_stop(h)

    def second_stops():
        for h in range(PARTS // 2):
            with span(f"second{h}"):
                second_stop(h)

    with span("sendblocks"):
        for i in range(nt - 1):
            send_blocks(i)
        keep_blocks()
    pl.when(early)(second_stops)
    with span("sendlast"):
        send_blocks(nt - 1)
    pl.when(jnp.logical_not(early))(second_stops)
    for h in range(PARTS // 2, PARTS):
        with span(f"second{h}"):
            second_stop(h)

    inv_one = 1.0 / (1.0 - 0.9**STEP)
    inv_two = 1.0 / (1.0 - 0.95**STEP)

    def adam(h, scales, tops):
        if h * RELAYS % PARTS == 0:
            r = h * RELAYS // PARTS
            with span(f"waitblocks{r}"):
                if r == 0:
                    drain(xr_s, rs.at[0])
                drain(xr_m.at[r], rm.at[r])
                drain(xr_c.at[r], rc.at[r])
            xf_m[r] = xr_m[r].astype(jnp.float32).reshape(slots * cp, LANES)
            xf_c[r] = xr_c[r].astype(jnp.float32).reshape(slots * 2 * cp, LANES)
        if scales is None:
            held = xr_s[:, 0, :]
            scales = held[:, 0:1], held[:, LANES // 4:LANES // 4 + 1], held[:, LANES // 2:LANES // 2 + 1]
        s1, s2, s0 = scales
        keep, q1, r1, t1, u1, q2, r2, t2, u2, mine = setup(h)
        with span(f"waitsecond{h}"):
            drain(r2, r2nd.at[h])
            drain(u2, u2nd.at[h])
        top1, top2 = tops
        more = [as_col(u2[b, :, :slots]) for b in range(r2.shape[0])]
        for i in range(h * cq, (h + 1) * cq):
            at = slice(i * LANES, (i + 1) * LANES)
            r, j = i // cp, i % cp
            near = slice((i - h * cq) * LANES, (i - h * cq + 1) * LANES)
            grad = keep[mine, :, near]
            for b in range(r2.shape[0]):
                grad = grad + r2[b, :, near].astype(jnp.float32) * more[b]
            first = xf_c[r, pl.ds(j, slots, stride=2 * cp), :] * s1
            other = xf_c[r, pl.ds(cp + j, slots, stride=2 * cp), :] * s2
            old = xf_m[r, pl.ds(j, slots, stride=cp), :] * s0
            one = 0.9 * first + 0.1 * grad
            two = 0.95 * other + 0.05 * grad * grad
            update = (one * inv_one) / (jnp.sqrt(two * inv_two) + 1e-08) + 0.1 * old
            new = old - 0.01 * update
            nm_out[0, :, at] = new
            wg[0, my_dp, :, at] = new.astype(jnp.bfloat16)
            m1_v[:, at] = one
            m2_v[:, at] = two
            top1 = jnp.maximum(top1, jnp.abs(one))
            top2 = jnp.maximum(top2, jnp.abs(two))
        return scales, (top1, top2)

    def gathered(chip, h):
        return wg.at[0, chip * 2 + my_c, :, cols(h)]

    def to_chip(h, chip, y, x):
        item = gathered(chip, h)
        pltpu.make_async_remote_copy(
            src_ref=item, dst_ref=item, send_sem=sent.at[12], recv_sem=ra.at[h, chip],
            device_id=(dp_of(y, x, my_c), my_t), device_id_type=MESH,
        ).start()

    def to_partner(h, chip):
        item = gathered(chip, h)
        pltpu.make_async_remote_copy(
            src_ref=item, dst_ref=item, send_sem=sent.at[12], recv_sem=rf.at[0],
            device_id=(partner, my_t), device_id_type=MESH,
        ).start()

    def arrived(h, chip):
        item = gathered(chip, h)
        pltpu.make_async_copy(item, item, ra.at[h, chip]).wait()

    rows_away = [row_away(away) for away in range(1, ny)]
    beside = my_y * 2 + other_x
    above = [y * 2 + my_x for y in rows_away]
    corners = [y * 2 + other_x for y in rows_away]

    def direct(h):
        return 2 * h >= PARTS

    def spread(h):
        to_chip(h, my_chip, my_y, other_x)
        for y in rows_away:
            to_chip(h, my_chip, y, my_x)
        if direct(h):
            for y in rows_away:
                to_chip(h, my_chip, y, other_x)
        to_partner(h, my_chip)

    def landed(h, chip):
        with span(f"arrive{h}"):
            arrived(h, chip)
        to_partner(h, chip)

    def relay(h):
        if direct(h):
            for chip in [beside] + above:
                landed(h, chip)
        elif h % 2 == 0:
            for chip in above:
                with span(f"relay{h}"):
                    arrived(h, chip)
                to_chip(h, chip, my_y, other_x)
                to_partner(h, chip)
            landed(h, beside)
        else:
            with span(f"relay{h}"):
                arrived(h, beside)
            for y in rows_away:
                to_chip(h, beside, y, my_x)
            to_partner(h, beside)
            for chip in above:
                landed(h, chip)

    def finish(h):
        for chip in corners:
            landed(h, chip)

    zero = jnp.zeros((slots, LANES), jnp.float32)
    scales, tops = None, (zero, zero)
    for h in range(PARTS):
        with span(f"adam{h}"):
            scales, tops = adam(h, scales, tops)
        with span(f"spread{h}"):
            spread(h)
    with span("codes"):
        top1 = jnp.max(tops[0], axis=1, keepdims=True) + 1e-06
        top2 = jnp.max(tops[1], axis=1, keepdims=True) + 1e-06
        ns1_out[...] = as_row(top1)
        ns2_out[...] = as_row(top2)
        inv1 = 1.0 / top1
        inv2 = 1.0 / top2
        for j in range(chunks):
            at = slice(j * LANES, (j + 1) * LANES)
            nc1_out[0, :, at] = (m1_v[:, at] * inv1).astype(jnp.bfloat16)
            nc2_out[0, :, at] = (m2_v[:, at] * inv2).astype(jnp.bfloat16)

    for h in range(PARTS):
        relay(h)
    with span("finish"):
        for h in range(PARTS):
            finish(h)
    with span("drainend"):
        drain(wg.at[0, pl.ds(0, chips)], rf.at[0])
        rest = pl.ds(0, slots - per)
        items = (got, q1_x, q1_y, t1_x, t1_y, q2_x, q2_y, t2_x, t2_y,
                 xs_m.at[:, rest], xs_c.at[:, rest], xs_s.at[rest], wg.at[0, pl.ds(0, 2 * chips - 1)])
        for i, item in enumerate(items):
            drain(item, sent.at[i])


def _write_out(*refs):
    sem = refs[-1]
    count = (len(refs) - 1) // 2
    copies = [pltpu.make_async_copy(refs[i], refs[count + i], sem.at[i]) for i in range(count)]
    for item in copies:
        item.start()
    for item in copies:
        item.wait()


def _bytes(shape, dtype):
    return math.prod(shape) * jnp.dtype(dtype).itemsize


def on_device(send_order, master, first_code, first_scale, second_code, second_scale, grads):
    arrays = (send_order, master, first_code, first_scale, second_code, second_scale, grads)
    nd = lax.axis_size("dp")
    nt = lax.axis_size("tensor")
    slots = master.shape[1]
    width = master.shape[2]
    f32, b16, i16 = jnp.float32, jnp.bfloat16, jnp.int16
    dma = pltpu.SemaphoreType.DMA
    ny = nd // 4
    pairs = PARTS // 2
    wp = width // PARTS
    cp = width // LANES // RELAYS
    arrays = arrays[:6] + (grads.reshape(ny, 2, 2, slots, width),)
    results = (
        ((1, slots, width), f32),
        ((1, slots, width), b16),
        ((1, slots), f32),
        ((1, slots, width), b16),
        ((1, slots), f32),
        ((1, nd, slots, width), b16),
    )
    first_x, first_y = (pairs, 1, ny), (pairs, ny - 1, 2)
    then_x, then_y = (pairs, ny - 1), (pairs, 1)
    data = [(lead + (slots, wp), i16) for lead in (first_x, first_y, first_x, first_y, then_x, then_y, then_x, then_y)]
    sizes = [(lead + (1, LANES), f32) for lead in (first_x, first_y, first_x, first_y, then_x, then_y, then_x, then_y)]
    scratch = [
        ((1, slots), jnp.int32),
        ((1, slots), f32),
        ((1, slots), f32),
        ((slots, width), f32),
        ((slots, width), b16),
        ((slots, width), b16),
        ((RELAYS, slots * cp, LANES), f32),
        ((RELAYS, slots * 2 * cp, LANES), f32),
        ((RELAYS, slots, cp, LANES), i16),
        ((RELAYS, slots, 2 * cp, LANES), b16),
        ((slots, 1, LANES), f32),
        ((RELAYS, slots, cp, LANES), i16),
        ((RELAYS, slots, 2 * cp, LANES), b16),
        ((slots, 1, LANES), f32),
        ((ny, 2, slots, width), b16),
        ((PARTS, ny, 2, slots, wp), b16),
        ((pairs, ny, slots, wp), f32),
        ((pairs, 2, slots, wp), f32),
        *data,
        *sizes,
        ((slots, width), f32),
        ((slots, width), f32),
    ]
    grant = sum(_bytes(*item) for item in scratch) + sum(_bytes(*item) for item in results) + slots * 8192 + 6 * 1024 * 1024
    held = pl.pallas_call(
        functools.partial(_kernel, nd, nt, slots, width),
        out_shape=tuple(pltpu.VMEM(*item) for item in results),
        in_specs=[pl.BlockSpec(memory_space=pltpu.HBM)] * 7,
        out_specs=[pl.BlockSpec(memory_space=pltpu.VMEM)] * 6,
        scratch_shapes=[
            *(pltpu.VMEM(*item) for item in scratch),
            dma((6,)), dma((1,)), dma((13,)), dma((RELAYS,)), dma((RELAYS,)), dma((1,)), dma((PARTS,)),
            dma((PARTS,)), dma((PARTS,)), dma((PARTS,)), dma((PARTS,)), dma((PARTS, 2 * ny)), dma((1,)),
            pltpu.SemaphoreType.REGULAR((nt,)),
        ],
        compiler_params=pltpu.CompilerParams(collective_id=0, has_side_effects=True, vmem_limit_bytes=grant),
        name="relayout_adam",
    )(*(pltpu.with_memory_space_constraint(item, pltpu.HBM) for item in arrays))
    return pl.pallas_call(
        _write_out,
        out_shape=tuple(jax.ShapeDtypeStruct(*item) for item in results),
        in_specs=[pl.BlockSpec(memory_space=pltpu.VMEM)] * len(results),
        out_specs=[pl.BlockSpec(memory_space=pltpu.HBM)] * len(results),
        scratch_shapes=[dma((len(results),))],
        compiler_params=pltpu.CompilerParams(vmem_limit_bytes=2 * 1024 * 1024),
        name="write_out",
    )(*(pltpu.with_memory_space_constraint(item, pltpu.VMEM) for item in held))


def solution(mesh):
    placed = (
        P(("dp", "tensor"), None),
        P(("dp", "tensor"), None, None),
        P(("dp", "tensor"), None, None),
        P(("dp", "tensor"), None),
        P(("dp", "tensor"), None, None),
        P(("dp", "tensor"), None),
        P("dp", "tensor", None, None, None),
    )
    return jax.shard_map(
        on_device,
        mesh=mesh,
        in_specs=placed,
        out_specs=(
            P(("dp", "tensor"), None, None),
            P(("dp", "tensor"), None, None),
            P(("dp", "tensor"), None),
            P(("dp", "tensor"), None, None),
            P(("dp", "tensor"), None),
            P("tensor", None, None, None),
        ),
        check_vma=False,
    )
```
